32 devices in a mesh: dp: 16 (over z, x, core), tensor: 2 (over y).
Axes of the slice: x: 2, y: 2, z: 4, core: 2. Of those that a mesh axis runs over, the one named last changes fastest.
Arguments:
- tokens: bfloat16 [20480, 1024], P(('dp', 'tensor')), may hold values from -6 to 6
- lengths: int32 [16, 3], P('dp'), may hold values from 1 to 1024, 1280 in all within a row
- attention_norm1_gain: float32 [1024], replicated, may hold values from 0.5 to 1.5
- qkv_weight: bfloat16 [1024, 3, 1024], P('dp', None, 'tensor'), may hold values from -0.28125 to 0.28125
- out_weight: bfloat16 [1024, 1024], P('tensor', 'dp'), may hold values from -3 to 3
- feedforward_norm2_gain: float32 [1024], replicated, may hold values from 0.5 to 1.5
- up_weight: bfloat16 [1024, 2, 2624], P('dp', None, 'tensor'), may hold values from -0.1875 to 0.1875
- down_weight: bfloat16 [2624, 1024], P('tensor', 'dp'), may hold values from -0.125 to 0.125
- output_gradient: bfloat16 [20480, 1024], P(('dp', 'tensor')), may hold values from -6 to 6
Outputs:
- mixed: bfloat16 [20480, 1024], P(('dp', 'tensor'))
- token_gradients: float32 [20480, 1024], P(('dp', 'tensor'))
- grad_norm1_gain: float32 [1024], replicated
- grad_qkv: float32 [1024, 3, 1024], P('dp', None, 'tensor')
- grad_out_weight: float32 [1024, 1024], P('tensor', 'dp')
- grad_norm2_gain: float32 [1024], replicated
- grad_up: float32 [1024, 2, 2624], P('dp', None, 'tensor')
- grad_down: float32 [2624, 1024], P('tensor', 'dp')
The draws below stay inside these ranges and needn't reach their ends.
Inputs may be any that keep to these rules, and one draw needn't show every extreme that they name: `lengths`: each row sums to 1280, and its longest sequence has exactly 1024 tokens.
All inputs are finite; a program needn't handle non-finite values.
Results may differ from the reference program's by a relative error of at most 0.019.
Values may be sent and summed in bfloat16 or wider, within the bound.
No kernel may reach another device: no remote copies, remote signals or barrier semaphores. Data moves between devices by JAX's collectives and lax.ppermute only.
A program may use at most 256 MiB of HBM per device.

```python
import math
import jax
import jax.numpy as jnp
import numpy as np
from jax import lax

D = 1024
H = 16
DH = 64
FF = 2624
TOK_DP = 1280
SEQ_MAX = 1024
SEQS = 3
TOKENS = 20480
N_DP = 16


def draw_qkv_weight(key, part):
    sample_values = jnp.clip(jax.random.normal(key, (D, 3, D), jnp.float32), -6.0, 6.0) * D ** (-0.5)
    return sample_values.astype(jnp.bfloat16)


def shard_levels(stream_key, dims, cuts, smallest, high):
    def one(axis_at, shards_of):
        steps = jax.random.uniform(jax.random.fold_in(jax.random.fold_in(stream_key, 6), axis_at), (shards_of,), jnp.float32, smallest / len(cuts), high / len(cuts))
        return jnp.repeat(jnp.exp(steps), dims[axis_at] // shards_of).reshape((-1,) + (1,) * (len(dims) - axis_at - 1))

    level = one(*cuts[0])
    for cut in cuts[1:]:
        level = level * one(*cut)
    return level


def length_profile(amount, total, bound, lean):
    portions = [(1 << 20) // math.isqrt(rank ** lean) + 1 for rank in range(2, amount + 1)]
    surplus, given = total - bound - (amount - 1), [1] * (amount - 1)
    while surplus > 0:
        movable = [i for i in range(amount - 1) if given[i] < bound]
        pool, budget = sum([portions[i] for i in movable]), surplus
        for i in movable:
            addition = min(bound - given[i], max(1, budget * portions[i] // pool), surplus)
            given[i] = given[i] + addition
            surplus = surplus - addition
    return np.array([bound] + given)


def ragged_sizes(own_key, amount, total, most, skew):
    if amount == 2:
        one = jax.random.randint(own_key, (), max(1, total - most), min(most, total - 1) + 1)
        return jnp.stack([one, total - one])
    tallies = jnp.asarray(length_profile(amount, total, most, skew), jnp.int32)
    pairs = (amount - 1) // 2
    source_of, taker = tallies[1:1 + 2 * pairs:2], tallies[2:2 + 2 * pairs:2]
    margin = jnp.minimum(source_of - 1, most - taker)
    shifted = jax.random.randint(jax.random.fold_in(own_key, 1), (pairs,), 0, 1 << 20) % (margin + 1)
    tallies = tallies.at[1:1 + 2 * pairs:2].set(source_of - shifted).at[2:2 + 2 * pairs:2].set(taker + shifted)
    return tallies[jax.random.permutation(jax.random.fold_in(own_key, 2), amount)]


def centred(rng, extent, scale, reach, split=(), kind=jnp.bfloat16):
    drawn = scale * jax.random.normal(rng, extent, jnp.float32)
    if split:
        drawn = drawn * shard_levels(rng, extent, split, -0.22, 0.18)
    return jnp.clip(drawn, -reach, reach).astype(kind)


def setup_inputs(seed: int = 0) -> dict:
    key_of = jax.random.split(jax.random.key(seed), 10)
    tokens = centred(key_of[0], (TOKENS, D), 1.0, 6.0, ((0, 32),))
    lengths = jax.vmap(lambda own: ragged_sizes(own, SEQS, TOK_DP, SEQ_MAX, 2))(jax.random.split(key_of[1], N_DP)).reshape((N_DP, SEQS)).astype(jnp.int32)
    attention_norm1_gain = jnp.clip(1.0 + 0.1 * jax.random.normal(key_of[2], (D,), jnp.float32), 0.5, 1.5)
    qkv_weight = draw_qkv_weight(jax.random.fold_in(key_of[9], 71), 0)
    out_weight = centred(key_of[4], (D, D), (D * 4 // SEQ_MAX) ** -0.5, 3.0, ((0, 2), (1, 16)))
    feedforward_norm2_gain = jnp.clip(1.0 + 0.1 * jax.random.normal(key_of[5], (D,), jnp.float32), 0.5, 1.5)
    up_weight = centred(key_of[6], (D, 2, FF), D ** -0.5, 0.1875, ((0, 16), (2, 2)))
    down_weight = centred(key_of[7], (FF, D), FF ** -0.5, 0.125, ((0, 2), (1, 16)))
    output_gradient = centred(key_of[8], (TOKENS, D), 1.0, 6.0, ((0, 32),))
    return {"tokens": tokens, "lengths": lengths, "attention_norm1_gain": attention_norm1_gain, "qkv_weight": qkv_weight, "out_weight": out_weight, "feedforward_norm2_gain": feedforward_norm2_gain, "up_weight": up_weight, "down_weight": down_weight, "output_gradient": output_gradient}


ROPE_BASE = 160000.0
NORM_EPS = 1e-05
NEG_FILL = -1e+30

def rounded(values):
    return lax.optimization_barrier(values.astype(jnp.bfloat16)).astype(jnp.float32)

def rope_tables(lengths_row, count):
    ends = jnp.cumsum(lengths_row).astype(jnp.int32)
    places = jnp.arange(count, dtype=jnp.int32)
    segment_ids = lax.optimization_barrier(jnp.sum((places[:, None] >= ends[None, :]).astype(jnp.int32), axis=1)).astype(jnp.int32)
    starts = (ends - lengths_row).astype(jnp.int32)
    member = segment_ids[:, None] == jnp.arange(lengths_row.shape[0], dtype=jnp.int32)[None, :]
    firsts = lax.optimization_barrier(jnp.sum(jnp.where(member, starts[None, :], 0), axis=1)).astype(jnp.int32)
    offsets = (places - firsts).astype(jnp.float32)
    freqs = ROPE_BASE ** (-jnp.arange(0, DH, 2).astype(jnp.float32) / DH)
    angles = offsets[:, None] * freqs[None, :]
    cosine_table = jnp.concatenate([jnp.cos(angles), jnp.cos(angles)], axis=1)
    sine_table = jnp.concatenate([jnp.sin(angles), jnp.sin(angles)], axis=1)
    return (segment_ids, cosine_table, sine_table)

def turn_half(values):
    middle = values.shape[-1] // 2
    return jnp.concatenate([-values[..., middle:], values[..., :middle]], axis=-1)

def rotate_rows(values, cosine_table, sine_table):
    return values * cosine_table[:, None, :] + turn_half(values) * sine_table[:, None, :]

def unrotate_rows(values, cosine_table, sine_table):
    return values * cosine_table[:, None, :] - turn_half(values) * sine_table[:, None, :]

def apply_norm(values):
    center = values - lax.optimization_barrier(jnp.mean(values, axis=-1, keepdims=True))
    scale_back = lax.rsqrt(lax.optimization_barrier(jnp.mean(center * center, axis=-1, keepdims=True)) + NORM_EPS)
    return (center * scale_back, scale_back)

def norm_backward(grad_norm, normed, scale_back, gain):
    grad_hat = grad_norm * gain
    return scale_back * (grad_hat - lax.optimization_barrier(jnp.mean(grad_hat, axis=-1, keepdims=True)) - normed * lax.optimization_barrier(jnp.mean(grad_hat * normed, axis=-1, keepdims=True)))

def gelu_pair(values):
    cdf = 0.5 * (1.0 + jax.scipy.special.erf(values * 0.7071067811865476))
    density = jnp.exp(-0.5 * values * values) * 0.3989422804014327
    return (values * cdf, cdf + values * density)

def masked_scores(queries, keys, segment_ids):
    scores = jnp.einsum('qhd,khd->hqk', queries.astype(jnp.float32), keys.astype(jnp.float32)) * DH ** (-0.5)
    allowed = segment_ids[:, None] == segment_ids[None, :]
    return jnp.where(allowed[None], scores, NEG_FILL)

def one_group(token_rows, lengths_row, attention_norm1_gain, qkv_weight, out_weight, feedforward_norm2_gain, up_weight, down_weight, row_gradients):
    count = token_rows.shape[0]
    segment_ids, cosine_table, sine_table = rope_tables(lengths_row, count)
    input_rows = token_rows.astype(jnp.float32)
    centered_scaled1, inverse_deviation1 = apply_norm(input_rows)
    hidden_first = (centered_scaled1 * attention_norm1_gain).astype(jnp.bfloat16)
    projected = jnp.einsum('td,dch->tch', hidden_first.astype(jnp.float32), qkv_weight.astype(jnp.float32))
    queries = rotate_rows(projected[:, 0].reshape(count, H, DH), cosine_table, sine_table).astype(jnp.bfloat16)
    keys = rotate_rows(projected[:, 1].reshape(count, H, DH), cosine_table, sine_table).astype(jnp.bfloat16)
    values = projected[:, 2].reshape(count, H, DH).astype(jnp.bfloat16)
    scores = masked_scores(queries, keys, segment_ids)
    peak = lax.optimization_barrier(jnp.max(scores, axis=-1, keepdims=True))
    log_totals = peak + jnp.log(lax.optimization_barrier(jnp.sum(jnp.exp(scores - peak), axis=-1, keepdims=True)))
    probs = jnp.exp(scores - log_totals)
    attended = jnp.einsum('hqk,khd->qhd', rounded(probs), values.astype(jnp.float32)).astype(jnp.bfloat16)
    attended_flat = attended.reshape(count, H * DH)
    residual_stream = input_rows + jnp.dot(attended_flat, out_weight, preferred_element_type=jnp.float32)
    centered_scaled2, inverse_deviation2 = apply_norm(residual_stream)
    hidden_second = (centered_scaled2 * feedforward_norm2_gain).astype(jnp.bfloat16)
    lifted = jnp.einsum('td,dch->tch', hidden_second.astype(jnp.float32), up_weight.astype(jnp.float32))
    gelu_value, gelu_slope = gelu_pair(lifted[:, 0])
    act = (gelu_value * lifted[:, 1]).astype(jnp.bfloat16)
    mixed = (residual_stream + jnp.dot(act, down_weight, preferred_element_type=jnp.float32)).astype(jnp.bfloat16)
    grad_down = jnp.dot(act.T, row_gradients, preferred_element_type=jnp.float32)
    grad_act = jnp.dot(row_gradients, down_weight.T, preferred_element_type=jnp.float32)
    grad_lift = jnp.stack([grad_act * lifted[:, 1] * gelu_slope, grad_act * gelu_value], axis=1).astype(jnp.bfloat16)
    grad_up = jnp.einsum('td,tch->dch', hidden_second.astype(jnp.float32), grad_lift.astype(jnp.float32))
    second_hidden_gradient = jnp.einsum('tch,dch->td', grad_lift.astype(jnp.float32), up_weight.astype(jnp.float32))
    second_gain_gradient = lax.optimization_barrier(jnp.sum(second_hidden_gradient * centered_scaled2, axis=0))
    residual_gradient = row_gradients.astype(jnp.float32) + norm_backward(second_hidden_gradient, centered_scaled2, inverse_deviation2, feedforward_norm2_gain)
    grad_resid_low = residual_gradient.astype(jnp.bfloat16)
    grad_out_weight = jnp.dot(attended_flat.T, grad_resid_low, preferred_element_type=jnp.float32)
    grad_attended = jnp.dot(grad_resid_low, out_weight.T, preferred_element_type=jnp.float32).astype(jnp.bfloat16)
    grad_attended = grad_attended.reshape(count, H, DH).astype(jnp.float32)
    probs_low = rounded(probs)
    grad_values = jnp.einsum('hqk,qhd->khd', probs_low, grad_attended)
    grad_probs = jnp.einsum('qhd,khd->hqk', grad_attended, values.astype(jnp.float32))
    inner = lax.optimization_barrier(jnp.sum(grad_attended * attended.astype(jnp.float32), axis=-1)).T[:, :, None]
    grad_scores = rounded(probs * (grad_probs - inner))
    grad_queries = jnp.einsum('hqk,khd->qhd', grad_scores, keys.astype(jnp.float32)) * DH ** (-0.5)
    grad_keys = jnp.einsum('hqk,qhd->khd', grad_scores, queries.astype(jnp.float32)) * DH ** (-0.5)
    grad_queries = unrotate_rows(grad_queries, cosine_table, sine_table).astype(jnp.bfloat16)
    grad_keys = unrotate_rows(grad_keys, cosine_table, sine_table).astype(jnp.bfloat16)
    grad_projected = jnp.stack([grad_queries.reshape(count, H * DH), grad_keys.reshape(count, H * DH), grad_values.astype(jnp.bfloat16).reshape(count, H * DH)], axis=1)
    grad_qkv = jnp.einsum('td,tch->dch', hidden_first.astype(jnp.float32), grad_projected.astype(jnp.float32))
    first_hidden_gradient = jnp.einsum('tch,dch->td', grad_projected.astype(jnp.float32), qkv_weight.astype(jnp.float32))
    first_gain_gradient = lax.optimization_barrier(jnp.sum(first_hidden_gradient * centered_scaled1, axis=0))
    token_gradients = residual_gradient + norm_backward(first_hidden_gradient, centered_scaled1, inverse_deviation1, attention_norm1_gain)
    return (mixed, token_gradients, (first_gain_gradient, grad_qkv, grad_out_weight, second_gain_gradient, grad_up, grad_down))

def reference(tokens, lengths, attention_norm1_gain, qkv_weight, out_weight, feedforward_norm2_gain, up_weight, down_weight, output_gradient):
    token_groups = tokens.reshape(N_DP, TOK_DP, D)
    grad_groups = output_gradient.reshape(N_DP, TOK_DP, D)
    start_sums = (jnp.zeros((D,), jnp.float32), jnp.zeros((D, 3, D), jnp.float32), jnp.zeros((D, D), jnp.float32), jnp.zeros((D,), jnp.float32), jnp.zeros((D, 2, FF), jnp.float32), jnp.zeros((FF, D), jnp.float32))

    def visit(sums, item):
        token_rows, lengths_row, row_gradients = item
        mixed, token_gradients, grads = one_group(token_rows, lengths_row, attention_norm1_gain, qkv_weight, out_weight, feedforward_norm2_gain, up_weight, down_weight, row_gradients)
        sums = tuple((total + piece for total, piece in zip(sums, grads)))
        return (sums, (mixed, token_gradients))
    sums, (mixed, token_gradients) = lax.scan(visit, start_sums, (token_groups, lengths, grad_groups))
    return (mixed.reshape(TOKENS, D), token_gradients.reshape(TOKENS, D), sums[0], sums[1], sums[2], sums[3], sums[4], sums[5])
```

```python
import jax
import jax.numpy as jnp
from jax import lax
from jax.experimental import pallas as pl
from jax.experimental.pallas import tpu as pltpu
from jax.sharding import PartitionSpec as P

DH = 64


ROPE_BASE = 160000.0
NORM_EPS = 1e-05
NEG_FILL = -1e30


def sequence_ids(lengths_row, places):
    ends = jnp.cumsum(lengths_row)
    return jnp.sum((places[:, None] >= ends[None, :]).astype(jnp.int32), axis=1)


def rope_tables(lengths_row, places):
    ends = jnp.cumsum(lengths_row)
    segment_ids = sequence_ids(lengths_row, places)
    starts = ends - lengths_row
    member = segment_ids[:, None] == jnp.arange(lengths_row.shape[0], dtype=jnp.int32)[None, :]
    firsts = jnp.sum(jnp.where(member, starts[None, :], 0), axis=1)
    offsets = (places - firsts).astype(jnp.float32)
    freqs = ROPE_BASE ** (-jnp.arange(0, DH, 2).astype(jnp.float32) / DH)
    angles = offsets[:, None] * freqs[None, :]
    cosine, sine = jnp.cos(angles), jnp.sin(angles)
    return (
        jnp.concatenate([cosine, cosine, cosine, cosine], axis=1),
        jnp.concatenate([-sine, sine, -sine, sine], axis=1),
    )


def apply_norm(values):
    center = values - jnp.mean(values, axis=-1, keepdims=True)
    scale_back = lax.rsqrt(jnp.mean(center * center, axis=-1, keepdims=True) + NORM_EPS)
    return (center * scale_back, scale_back)


def norm_backward(grad_norm, normed, scale_back, gain):
    grad_hat = grad_norm * gain
    return scale_back * (
        grad_hat
        - jnp.mean(grad_hat, axis=-1, keepdims=True)
        - normed * jnp.mean(grad_hat * normed, axis=-1, keepdims=True)
    )


def gelu_pair(values):
    cdf = 0.5 * (1.0 + jax.scipy.special.erf(values * 0.7071067811865476))
    density = jnp.exp(-0.5 * values * values) * 0.3989422804014327
    return (values * cdf, cdf + values * density)


LONG = 1024
QUERY_BLOCK = 256


def head_lanes(rows):
    return lax.broadcasted_iota(jnp.int32, (rows, 2 * DH), 1)


def turn_lanes(values):
    lanes = head_lanes(values.shape[0]) % DH
    return jnp.where(
        lanes < DH // 2,
        pltpu.roll(values, 2 * DH - DH // 2, 1),
        pltpu.roll(values, DH // 2, 1),
    )


def roll_rows(values, twice_ref, first):
    rows = values.shape[0]
    twice_ref[:rows] = values
    twice_ref[rows:] = values
    return twice_ref[pl.ds(first, rows), :]


def only_head(values, head):
    lanes = head_lanes(values.shape[0])
    return jnp.where((lanes >= head * DH) & (lanes < (head + 1) * DH), values, 0)


def dot_rows(left, right):
    return lax.dot_general(
        left, right, (((1,), (1,)), ((), ())), preferred_element_type=jnp.float32
    )


def dot_plain(left, right):
    return lax.dot_general(
        left, right, (((1,), (0,)), ((), ())), preferred_element_type=jnp.float32
    )


def query_spans(rows):
    spans = [(first, QUERY_BLOCK, 0, LONG) for first in range(0, LONG, QUERY_BLOCK)]
    return spans + [(LONG, rows - LONG, LONG, rows - LONG)]


def forward_kernel(
    shift_ref, q_raw, k_raw, v_raw, cos_ref, sin_ref, ids_col, ids_row,
    q_out, k_out, v_out, att_out, lse_out, twice, att_scr,
):
    rows = q_raw.shape[0]
    shift = shift_ref[0]
    cos, sin = cos_ref[...], sin_ref[...]
    q = q_raw[...]
    q = roll_rows(q * cos + turn_lanes(q) * sin, twice, shift).astype(jnp.bfloat16) * 0.125
    q = q.astype(jnp.bfloat16)
    q_out[...] = q
    k = k_raw[...]
    k = roll_rows(k * cos + turn_lanes(k) * sin, twice, shift).astype(jnp.bfloat16)
    k_out[...] = k
    v = roll_rows(v_raw[...], twice, shift)
    v_out[...] = v.astype(jnp.bfloat16)
    v_t = v.T.astype(jnp.bfloat16)
    for first, count, key_first, key_count in query_spans(rows):
        block = q_out[first : first + count]
        pieces = []
        for head in range(2):
            scores = dot_rows(k_out[key_first : key_first + key_count], only_head(block, head))
            if key_first:
                scores = jnp.where(ids_col[...] == ids_row[...], scores, NEG_FILL)
            peak = jnp.max(scores, axis=0, keepdims=True)
            weights = jnp.exp(scores - peak)
            total = jnp.sum(weights, axis=0, keepdims=True)
            lse_out[0, head : head + 1, first : first + count] = peak + jnp.log(total)
            piece = dot_plain(
                v_t[head * DH : (head + 1) * DH, key_first : key_first + key_count],
                weights.astype(jnp.bfloat16),
            )
            pieces.append(piece / total)
        att_scr[first : first + count] = jnp.concatenate(pieces, axis=0).T
    back = lax.rem(rows - shift, rows)
    att_out[...] = roll_rows(att_scr[...], twice, back).astype(jnp.bfloat16)


def backward_kernel(
    shift_ref, q_ref, k_ref, v_ref, grad_ref, att_ref, lse_ref, cos_ref, sin_ref, ids_col, ids_row,
    dq_out, dk_out, dv_out, twice, grad_scr, inner_scr, key_t, dq_scr, dk_scr, dv_scr,
):
    rows = q_ref.shape[0]
    shift = shift_ref[0]
    grad = grad_ref[...].astype(jnp.float32)
    products = roll_rows(grad * att_ref[...].astype(jnp.float32), twice, shift).T
    inner_scr[0:1] = jnp.sum(products[:DH], axis=0, keepdims=True)
    inner_scr[1:2] = jnp.sum(products[DH:], axis=0, keepdims=True)
    grad_scr[...] = roll_rows(grad, twice, shift).astype(jnp.bfloat16)
    key_t[...] = k_ref[...].astype(jnp.float32).T.astype(jnp.bfloat16)
    for first, count, key_first, key_count in query_spans(rows):
        keys = slice(key_first, key_first + key_count)
        block = slice(first, first + count)
        pieces, probs_low, scores_low, queries_head, grads_head = [], [], [], [], []
        for head in range(2):
            q_head = only_head(q_ref[block], head)
            g_head = only_head(grad_scr[block], head)
            scores = dot_rows(k_ref[keys], q_head)
            probs = jnp.exp(scores - lse_ref[0, head : head + 1, block])
            if key_first:
                probs = jnp.where(ids_col[...] == ids_row[...], probs, 0.0)
            grad_probs = dot_rows(v_ref[keys], g_head)
            grad_scores = probs * (grad_probs - inner_scr[head : head + 1, block])
            grad_scores = grad_scores.astype(jnp.bfloat16)
            pieces.append(dot_plain(key_t[head * DH : (head + 1) * DH, keys], grad_scores))
            probs_low.append(probs.astype(jnp.bfloat16))
            scores_low.append(grad_scores)
            queries_head.append(q_head)
            grads_head.append(g_head)
        dv_part = dot_plain(
            jnp.concatenate(probs_low, axis=1), jnp.concatenate(grads_head, axis=0)
        )
        dk_part = dot_plain(
            jnp.concatenate(scores_low, axis=1), jnp.concatenate(queries_head, axis=0)
        )
        if first % LONG == 0:
            dv_scr[keys] = dv_part
            dk_scr[keys] = dk_part
        else:
            dv_scr[keys] = dv_scr[keys] + dv_part
            dk_scr[keys] = dk_scr[keys] + dk_part
        dq_scr[block] = jnp.concatenate(pieces, axis=0).T * 0.125
    back = lax.rem(rows - shift, rows)
    cos, sin = cos_ref[...], sin_ref[...]
    dq = roll_rows(dq_scr[...], twice, back)
    dq_out[...] = (dq * cos - turn_lanes(dq) * sin).astype(jnp.bfloat16)
    dk = roll_rows(dk_scr[...], twice, back)
    dk_out[...] = (dk * cos - turn_lanes(dk) * sin).astype(jnp.bfloat16)
    dv_out[...] = roll_rows(dv_scr[...], twice, back).astype(jnp.bfloat16)


def attention_forward(projected, tables, shift, rest_ids):
    rows = projected.shape[0]
    pairs = projected.shape[1] // (6 * DH)
    pair = (rows, 2 * DH)
    rest = rows - LONG
    flat = jax.ShapeDtypeStruct((rows, pairs * 2 * DH), jnp.bfloat16)
    spec = pl.BlockSpec(pair, lambda p, s: (0, p))
    whole = lambda shape: pl.BlockSpec(shape, lambda p, s: (0, 0))
    return pl.pallas_call(
        forward_kernel,
        grid_spec=pltpu.PrefetchScalarGridSpec(
            num_scalar_prefetch=1,
            grid=(pairs,),
            in_specs=[
                spec,
                pl.BlockSpec(pair, lambda p, s: (0, pairs + p)),
                pl.BlockSpec(pair, lambda p, s: (0, 2 * pairs + p)),
                whole(pair),
                whole(pair),
                whole((rest, 1)),
                whole((1, rest)),
            ],
            out_specs=[spec, spec, spec, spec, pl.BlockSpec((1, 2, rows), lambda p, s: (p, 0, 0))],
            scratch_shapes=[
                pltpu.VMEM((2 * rows, 2 * DH), jnp.float32),
                pltpu.VMEM(pair, jnp.float32),
            ],
        ),
        out_shape=[flat, flat, flat, flat, jax.ShapeDtypeStruct((pairs, 2, rows), jnp.float32)],
        compiler_params=pltpu.CompilerParams(vmem_limit_bytes=48 << 20),
        name="attention_forward",
    )(shift, projected, projected, projected, *tables, rest_ids[:, None], rest_ids[None, :])


def attention_backward(
    queries, keys, values, grads, attended, lse, tables, shift, rest_ids, first_pair, pairs
):
    rows = queries.shape[0]
    pair = (rows, 2 * DH)
    rest = rows - LONG
    flat = jax.ShapeDtypeStruct((rows, pairs * 2 * DH), jnp.bfloat16)
    spec = pl.BlockSpec(pair, lambda p, s: (0, first_pair + p))
    out_spec = pl.BlockSpec(pair, lambda p, s: (0, p))
    whole = lambda shape: pl.BlockSpec(shape, lambda p, s: (0, 0))
    return pl.pallas_call(
        backward_kernel,
        grid_spec=pltpu.PrefetchScalarGridSpec(
            num_scalar_prefetch=1,
            grid=(pairs,),
            in_specs=[
                spec,
                spec,
                spec,
                spec,
                spec,
                pl.BlockSpec((1, 2, rows), lambda p, s: (first_pair + p, 0, 0)),
                whole(pair),
                whole(pair),
                whole((rest, 1)),
                whole((1, rest)),
            ],
            out_specs=[out_spec, out_spec, out_spec],
            scratch_shapes=[
                pltpu.VMEM((2 * rows, 2 * DH), jnp.float32),
                pltpu.VMEM(pair, jnp.bfloat16),
                pltpu.VMEM((8, rows), jnp.float32),
                pltpu.VMEM((2 * DH, rows), jnp.bfloat16),
                pltpu.VMEM(pair, jnp.float32),
                pltpu.VMEM(pair, jnp.float32),
                pltpu.VMEM(pair, jnp.float32),
            ],
        ),
        out_shape=[flat, flat, flat],
        compiler_params=pltpu.CompilerParams(vmem_limit_bytes=48 << 20),
        name="attention_backward",
    )(shift, queries, keys, values, grads, attended, lse, *tables, rest_ids[:, None], rest_ids[None, :])


def norm_rows(values):
    center = values - jnp.mean(values, axis=-1, keepdims=True)
    scale_back = lax.rsqrt(jnp.mean(center * center, axis=-1, keepdims=True) + NORM_EPS)
    return center * scale_back, scale_back


def residual_rows(x_ref, own_ref, other_ref):
    total = own_ref[...].astype(jnp.float32) + other_ref[...].astype(jnp.float32)
    return x_ref[...].astype(jnp.float32) + total


def feedforward_kernel(
    x_ref, own_ref, other_ref, grad_ref, gain_ref, weights_ref,
    h_out, act_out, lift_out, grad_h_out, mlp_out,
):
    padded = act_out.shape[1]
    up_ref, down_ref = weights_ref.at[:, : 2 * padded], weights_ref.at[:, 2 * padded :]
    normed, _ = norm_rows(residual_rows(x_ref, own_ref, other_ref))
    hidden = (normed * gain_ref[...]).astype(jnp.bfloat16)
    h_out[...] = hidden
    gate = dot_plain(hidden, up_ref[:, :padded])
    value = dot_plain(hidden, up_ref[:, padded:])
    grad_act = dot_plain(grad_ref[...], down_ref[...])
    gelu_value, gelu_slope = gelu_pair(gate)
    act = (gelu_value * value).astype(jnp.bfloat16)
    act_out[...] = act
    mlp_out[...] = dot_rows(act, down_ref[...]).astype(jnp.bfloat16)
    lift_out[:, :padded] = (grad_act * value * gelu_slope).astype(jnp.bfloat16)
    lift_out[:, padded:] = (grad_act * gelu_value).astype(jnp.bfloat16)
    grad_h_out[...] = dot_rows(lift_out[...], up_ref[...]).astype(jnp.bfloat16)


def middle_kernel(
    x_ref, own_ref, other_ref, gh_own_ref, gh_other_ref, grad_ref, gain_ref, out_ref,
    resid_out, low_out, att_out, gain_out,
):
    normed, scale_back = norm_rows(residual_rows(x_ref, own_ref, other_ref))
    grad_h = gh_own_ref[...].astype(jnp.float32) + gh_other_ref[...].astype(jnp.float32)
    result = grad_ref[...].astype(jnp.float32) + norm_backward(
        grad_h, normed, scale_back, gain_ref[...]
    )
    resid_out[...] = result
    low = result.astype(jnp.bfloat16)
    low_out[...] = low
    att_out[...] = dot_plain(low, out_ref[...]).astype(jnp.bfloat16)

    @pl.when(pl.program_id(0) == 0)
    def _():
        gain_out[...] = jnp.zeros_like(gain_out)

    gain_out[...] = gain_out[...] + jnp.sum(grad_h * normed, axis=0, keepdims=True)


def first_hidden_kernel(x_ref, weights_ref, *refs):
    part_refs, (partial_out, gain_out) = refs[:-2], refs[-2:]
    normed, _ = norm_rows(x_ref[...].astype(jnp.float32))
    grads = jnp.concatenate([ref[...] for ref in part_refs], axis=1)
    partial = dot_rows(grads, weights_ref[...])
    partial_out[...] = partial.astype(jnp.bfloat16)

    @pl.when(pl.program_id(0) == 0)
    def _():
        gain_out[...] = jnp.zeros_like(gain_out)

    gain_out[...] = gain_out[...] + jnp.sum(partial * normed, axis=0, keepdims=True)


def first_hidden(x, weights, parts, first_row):
    rows, width = x.shape
    tile = row_tile(rows)
    skip = first_row // tile
    return pl.pallas_call(
        first_hidden_kernel,
        grid=(rows // tile,),
        in_specs=[pl.BlockSpec((tile, width), lambda i: (i, 0)), fixed_block(weights.shape)]
        + [pl.BlockSpec((tile, part.shape[1]), lambda i: (skip + i, 0)) for part in parts],
        out_specs=[
            pl.BlockSpec((tile, width), lambda i: (i, 0)),
            pl.BlockSpec((1, width), lambda i: (0, 0)),
        ],
        out_shape=[
            jax.ShapeDtypeStruct((rows, width), jnp.bfloat16),
            jax.ShapeDtypeStruct((1, width), jnp.float32),
        ],
        compiler_params=pltpu.CompilerParams(vmem_limit_bytes=48 << 20),
        name="first_hidden",
    )(x, weights, *parts)


def row_tile(rows):
    for tile in (320, 256, 160, 128, 64, 32, 16):
        if rows % tile == 0:
            return tile
    return rows


def fixed_block(shape):
    return pl.BlockSpec(shape, lambda i: (0, 0), pipeline_mode=pl.Buffered(1))


def feedforward(x, own, other, grads, gain, weights):
    rows, width = x.shape
    padded = weights.shape[1] // 3
    tile = row_tile(rows)
    spec = lambda columns: pl.BlockSpec((tile, columns), lambda i: (i, 0))
    out = lambda columns: jax.ShapeDtypeStruct((rows, columns), jnp.bfloat16)
    return pl.pallas_call(
        feedforward_kernel,
        grid=(rows // tile,),
        in_specs=[spec(width)] * 4
        + [fixed_block((1, width)), fixed_block(weights.shape)],
        out_specs=[spec(width), spec(padded), spec(2 * padded), spec(width), spec(width)],
        out_shape=[out(width), out(padded), out(2 * padded), out(width), out(width)],
        compiler_params=pltpu.CompilerParams(vmem_limit_bytes=56 << 20),
        name="feedforward",
    )(x, own, other, grads, gain[None, :], weights)


def middle(x, own, other, gh_own, gh_other, grads, gain, w_out_t):
    rows, width = x.shape
    columns = w_out_t.shape[1]
    tile = row_tile(rows)
    spec = lambda columns: pl.BlockSpec((tile, columns), lambda i: (i, 0))
    return pl.pallas_call(
        middle_kernel,
        grid=(rows // tile,),
        in_specs=[spec(width)] * 6 + [fixed_block((1, width)), fixed_block(w_out_t.shape)],
        out_specs=[
            spec(width),
            spec(width),
            spec(columns),
            pl.BlockSpec((1, width), lambda i: (0, 0)),
        ],
        out_shape=[
            jax.ShapeDtypeStruct((rows, width), jnp.float32),
            jax.ShapeDtypeStruct((rows, width), jnp.bfloat16),
            jax.ShapeDtypeStruct((rows, columns), jnp.bfloat16),
            jax.ShapeDtypeStruct((1, width), jnp.float32),
        ],
        compiler_params=pltpu.CompilerParams(vmem_limit_bytes=48 << 20),
        name="middle",
    )(x, own, other, gh_own, gh_other, grads, gain[None, :], w_out_t)


def swap_pairs(values):
    return lax.ppermute(values, "tensor", [(0, 1), (1, 0)])


def gather_rows(values):
    if lax.axis_size("tensor") == 2:
        return [values, swap_pairs(values)]
    rows = values.shape[0]
    every = lax.all_gather(values, "tensor", axis=0, tiled=True)
    index = lax.axis_index("tensor")
    own_first = jnp.roll(every, -index * rows, axis=0)
    return [own_first[:rows], own_first[rows:]]


def sum_over_tensor(own, other):
    if lax.axis_size("tensor") == 2:
        first = swap_pairs(other)
        own_late, first = lax.optimization_barrier((own, first))
        return [first, swap_pairs(own_late)]
    rows, index = own.shape[0], lax.axis_index("tensor")
    full = jnp.roll(jnp.concatenate([own, other], axis=0), index * rows, axis=0)
    full = lax.psum(full, "tensor")
    full = jnp.roll(full, -index * rows, axis=0)
    return [full[:rows] - own, full[rows:] - other]


def exchange_both(own, other):
    if lax.axis_size("tensor") == 2:
        first = swap_pairs(own)
        other_late, first = lax.optimization_barrier((other, first))
        return [swap_pairs(other_late), first]
    return sum_over_tensor(own, other)


def receive_own(own, other):
    if lax.axis_size("tensor") == 2:
        return swap_pairs(other).astype(jnp.float32)
    rows, index = own.shape[0], lax.axis_index("tensor")
    full = jnp.roll(jnp.concatenate([own, other], axis=0), index * rows, axis=0)
    total = lax.psum_scatter(full, "tensor", scatter_dimension=0, tiled=True)
    return total.astype(jnp.float32) - own.astype(jnp.float32)


def sum_everywhere(values):
    total = lax.axis_size("dp") * lax.axis_size("tensor")
    if total & (total - 1):
        return lax.psum(values, ("dp", "tensor"))
    step = 1
    while step < total:
        pairs = [(i, i ^ step) for i in range(total)]
        values = values + lax.ppermute(values, ("dp", "tensor"), pairs)
        step *= 2
    return values


def gather_weights(shard):
    return lax.all_gather(shard, "dp", axis=0, tiled=True)


def exchange_bit(values, bit):
    size = lax.axis_size("dp")
    return lax.ppermute(values, "dp", [(i, i ^ bit) for i in range(size)])


def gather_doubling(shard):
    size, index = lax.axis_size("dp"), lax.axis_index("dp")
    if size & (size - 1):
        return gather_weights(shard)
    rows, columns = shard.shape
    state, bit = shard[None], size // 2
    while bit:
        received = exchange_bit(state, bit)
        high = (index // bit) % 2 == 1
        both = [jnp.where(high, received, state), jnp.where(high, state, received)]
        state = jnp.stack(both, axis=1).reshape(-1, rows, columns)
        bit //= 2
    return state.reshape(size * rows, columns)


def scatter_halving(full):
    size, index = lax.axis_size("dp"), lax.axis_index("dp")
    if size & (size - 1):
        return scatter_sums(full).astype(jnp.float32)
    rows, columns = full.shape[0] // size, full.shape[1]
    state, bit = full, 1
    while bit < size:
        halves = state.astype(jnp.bfloat16).reshape(-1, 2, rows, columns)
        mine = (index // bit) % 2
        received = exchange_bit(
            lax.dynamic_index_in_dim(halves, 1 - mine, axis=1, keepdims=False), bit
        )
        kept = lax.dynamic_index_in_dim(halves, mine, axis=1, keepdims=False)
        state = kept.astype(jnp.float32) + received.astype(jnp.float32)
        bit *= 2
    return state.reshape(rows, columns)


def scatter_sums(full):
    return lax.psum_scatter(full, "dp", scatter_dimension=0, tiled=True)


def matmul_low(equation, left, right):
    product = jnp.einsum(equation, left, right, preferred_element_type=jnp.float32)
    return product.astype(jnp.bfloat16)


def local(
    tokens,
    lengths,
    attention_norm1_gain,
    qkv_weight,
    out_weight,
    feedforward_norm2_gain,
    up_weight,
    down_weight,
    output_gradient,
):
    own_rows = tokens.shape[0]
    group_rows = own_rows * lax.axis_size("tensor")
    shard_rows, width = qkv_weight.shape[0], qkv_weight.shape[2]
    hidden = up_weight.shape[2]
    padded = -(-hidden // 128) * 128
    w_qkv = gather_weights(qkv_weight.reshape(shard_rows, 3 * width))
    up_shard = jnp.pad(up_weight, ((0, 0), (0, 0), (0, padded - hidden)))
    down_shard = jnp.pad(down_weight.T, ((0, 0), (0, padded - hidden)))
    w_ffn = gather_weights(
        jnp.concatenate([up_shard.reshape(shard_rows, 2 * padded), down_shard], axis=1)
    )
    w_out_t = gather_doubling(out_weight.T)

    first_place = lax.axis_index("tensor") * own_rows
    places = (jnp.arange(group_rows, dtype=jnp.int32) + first_place) % group_rows
    tables = rope_tables(lengths[0], places)
    long_start = jnp.sum(
        jnp.where(lengths[0] == LONG, jnp.cumsum(lengths[0]) - lengths[0], 0)
    ).astype(jnp.int32)
    shift = ((long_start - first_place) % group_rows).astype(jnp.int32).reshape(1)
    rest_places = (long_start + jnp.arange(LONG, group_rows, dtype=jnp.int32)) % group_rows
    rest_ids = sequence_ids(lengths[0], rest_places)

    token_parts = gather_rows(tokens)
    normed = [apply_norm(part.astype(jnp.float32)) for part in token_parts]
    h_one_all = jnp.concatenate(
        [(values * attention_norm1_gain).astype(jnp.bfloat16) for values, _ in normed], axis=0
    )
    projected = jnp.dot(h_one_all, w_qkv, preferred_element_type=jnp.float32)
    queries, keys, values, attended, lse = attention_forward(projected, tables, shift, rest_ids)
    grad_parts = gather_rows(lax.optimization_barrier((output_gradient, projected))[0])

    attn_other = matmul_low("th,dh->td", attended[own_rows:], w_out_t)
    attn_own = matmul_low("th,dh->td", attended[:own_rows], w_out_t)
    own_parts = [attn_own, attn_other]
    received = sum_over_tensor(attn_own, attn_other)

    def feed(index):
        return feedforward(
            token_parts[index],
            own_parts[index],
            received[index],
            grad_parts[index],
            feedforward_norm2_gain,
            w_ffn,
        )

    fed = [feed(0), feed(1)]
    h_two, act, grad_lift, grad_h2, mlp = [list(pair) for pair in zip(*fed)]
    gh_received = exchange_both(grad_h2[0], grad_h2[1])
    join = lambda pair: jnp.concatenate(pair, axis=0)
    grad_rows_all = join(grad_parts)
    grad_down_full = matmul_low("td,tf->df", grad_rows_all, join(act))
    grad_up_full = matmul_low("td,th->dh", join(h_two), join(grad_lift))
    ffn_sums = jnp.concatenate([grad_up_full, grad_down_full], axis=1)
    ffn_sums, gh_received[1] = lax.optimization_barrier((ffn_sums, gh_received[1]))
    ffn_part = scatter_sums(ffn_sums)

    mids = [
        middle(
            token_parts[index],
            own_parts[index],
            received[index],
            grad_h2[index],
            gh_received[index],
            grad_parts[index],
            feedforward_norm2_gain,
            w_out_t,
        )
        for index in range(2)
    ]
    residual_gradient, gain_gradient_second = mids[0][0], mids[0][3][0]
    grad_resid_all = join([mids[0][1], mids[1][1]])
    grad_attended = join([mids[0][2], mids[1][2]])
    mlp[1] = lax.optimization_barrier((mlp[1], gh_received[1]))[0]
    mlp_received = receive_own(mlp[0], mlp[1])

    pairs = width // (2 * DH)
    calls = 2 if pairs % 2 == 0 else 1
    grad_pieces, sums = [], []
    for call in range(calls):
        piece = attention_backward(
            queries,
            keys,
            values,
            grad_attended,
            attended,
            lse,
            tables,
            shift,
            rest_ids,
            call * (pairs // calls),
            pairs // calls,
        )
        grad_pieces.append(piece)
        columns = matmul_low("td,tc->dc", h_one_all, jnp.concatenate(piece, axis=1))
        if call == 0:
            grad_out_full = matmul_low("td,th->dh", grad_resid_all, attended)
            columns = jnp.concatenate([columns, grad_out_full], axis=1)
            if calls == 2:
                columns, grad_attended, mlp_received = lax.optimization_barrier(
                    (columns, grad_attended, mlp_received)
                )
        sums.append(scatter_halving(columns))

    parts = [grad_pieces[call][which] for which in range(3) for call in range(calls)]
    grad_h1_other, gain_other = first_hidden(token_parts[1], w_qkv, parts, own_rows)
    grad_h1_own, gain_own = first_hidden(token_parts[0], w_qkv, parts, 0)
    first_hidden_gradient = grad_h1_own.astype(jnp.float32) + receive_own(
        grad_h1_own, grad_h1_other
    )
    gain_grads = sum_everywhere(
        jnp.concatenate([gain_own + gain_other, gain_gradient_second[None]], axis=0)
    )
    mixed = (
        tokens.astype(jnp.float32)
        + (attn_own.astype(jnp.float32) + received[0].astype(jnp.float32))
        + (mlp[0].astype(jnp.float32) + mlp_received)
    ).astype(jnp.bfloat16)
    own_scaled1, inverse_deviation1 = normed[0]
    token_gradients = residual_gradient + norm_backward(
        first_hidden_gradient, own_scaled1, inverse_deviation1, attention_norm1_gain
    )
    ffn_part = ffn_part.astype(jnp.float32)
    qkv_part = jnp.concatenate(
        [
            part[:, : 3 * width // calls].reshape(shard_rows, 3, width // calls)
            for part in sums
        ],
        axis=2,
    )
    return (
        mixed,
        token_gradients,
        gain_grads[0],
        qkv_part,
        sums[0][:, 3 * width // calls :].T,
        gain_grads[1],
        ffn_part[:, : 2 * padded].reshape(shard_rows, 2, padded)[:, :, :hidden],
        ffn_part[:, 2 * padded : 2 * padded + hidden].T,
    )


def solution(mesh):
    return jax.shard_map(
        local,
        mesh=mesh,
        in_specs=(
            P(("dp", "tensor"), None),
            P("dp", None),
            P(),
            P("dp", None, "tensor"),
            P("tensor", "dp"),
            P(),
            P("dp", None, "tensor"),
            P("tensor", "dp"),
            P(("dp", "tensor"), None),
        ),
        out_specs=(
            P(("dp", "tensor"), None),
            P(("dp", "tensor"), None),
            P(),
            P("dp", None, "tensor"),
            P("tensor", "dp"),
            P(),
            P("dp", None, "tensor"),
            P("tensor", "dp"),
        ),
        check_vma=False,
    )
```

```python
import jax
import jax.numpy as jnp
from jax import lax
from jax.experimental import pallas as pl
from jax.experimental.pallas import tpu as pltpu
from jax.sharding import PartitionSpec as P


DH = 64


ROPE_BASE = 160000.0
NORM_EPS = 1e-05
NEG_FILL = -1e30


def sequence_ids(lengths_row, places):
    ends = jnp.cumsum(lengths_row)
    return jnp.sum((places[:, None] >= ends[None, :]).astype(jnp.int32), axis=1)


def rope_tables(lengths_row, places):
    ends = jnp.cumsum(lengths_row)
    segment_ids = sequence_ids(lengths_row, places)
    starts = ends - lengths_row
    member = segment_ids[:, None] == jnp.arange(lengths_row.shape[0], dtype=jnp.int32)[None, :]
    firsts = jnp.sum(jnp.where(member, starts[None, :], 0), axis=1)
    offsets = (places - firsts).astype(jnp.float32)
    freqs = ROPE_BASE ** (-jnp.arange(0, DH, 2).astype(jnp.float32) / DH)
    angles = offsets[:, None] * freqs[None, :]
    cosine, sine = jnp.cos(angles), jnp.sin(angles)
    return (
        jnp.concatenate([cosine, cosine, cosine, cosine], axis=1),
        jnp.concatenate([-sine, sine, -sine, sine], axis=1),
    )


def apply_norm(values):
    center = values - jnp.mean(values, axis=-1, keepdims=True)
    scale_back = lax.rsqrt(jnp.mean(center * center, axis=-1, keepdims=True) + NORM_EPS)
    return (center * scale_back, scale_back)


def norm_backward(grad_norm, normed, scale_back, gain):
    grad_hat = grad_norm * gain
    return scale_back * (
        grad_hat
        - jnp.mean(grad_hat, axis=-1, keepdims=True)
        - normed * jnp.mean(grad_hat * normed, axis=-1, keepdims=True)
    )


def gelu_pair(values):
    cdf = 0.5 * (1.0 + jax.scipy.special.erf(values * 0.7071067811865476))
    density = jnp.exp(-0.5 * values * values) * 0.3989422804014327
    return (values * cdf, cdf + values * density)


LONG = 1024
QUERY_BLOCK = 256


def head_lanes(rows):
    return lax.broadcasted_iota(jnp.int32, (rows, 2 * DH), 1)


def turn_lanes(values):
    lanes = head_lanes(values.shape[0]) % DH
    return jnp.where(
        lanes < DH // 2,
        pltpu.roll(values, 2 * DH - DH // 2, 1),
        pltpu.roll(values, DH // 2, 1),
    )


def roll_rows(values, twice_ref, first):
    rows = values.shape[0]
    twice_ref[:rows] = values
    twice_ref[rows:] = values
    return twice_ref[pl.ds(first, rows), :]


def only_head(values, head):
    lanes = head_lanes(values.shape[0])
    return jnp.where((lanes >= head * DH) & (lanes < (head + 1) * DH), values, 0)


def dot_rows(left, right):
    return lax.dot_general(
        left, right, (((1,), (1,)), ((), ())), preferred_element_type=jnp.float32
    )


def dot_plain(left, right):
    return lax.dot_general(
        left, right, (((1,), (0,)), ((), ())), preferred_element_type=jnp.float32
    )


def fold_rows(combine, values):
    while values.shape[0] % 16 == 0:
        half = values.shape[0] // 2
        values = combine(values[:half], values[half:])
    return values


def cost(flops, bytes_accessed, transcendentals=0):
    return pl.CostEstimate(
        flops=int(flops), bytes_accessed=int(bytes_accessed), transcendentals=int(transcendentals)
    )


def query_spans(rows):
    spans = [(first, QUERY_BLOCK, 0, LONG) for first in range(0, LONG, QUERY_BLOCK)]
    return spans + [(LONG, rows - LONG, LONG, rows - LONG)]


def forward_kernel(
    shift_ref, q_raw, k_raw, v_raw, cos_ref, sin_ref, ids_col, ids_row,
    q_out, k_out, v_out, att_out, lse_out, twice, att_scr,
):
    rows = q_raw.shape[0]
    shift = shift_ref[0]
    cos, sin = cos_ref[...], sin_ref[...]
    q = q_raw[...]
    q = roll_rows(q * cos + turn_lanes(q) * sin, twice, shift).astype(jnp.bfloat16) * 0.125
    q = q.astype(jnp.bfloat16)
    q_out[...] = q
    k = k_raw[...]
    k = roll_rows(k * cos + turn_lanes(k) * sin, twice, shift).astype(jnp.bfloat16)
    k_out[...] = k
    v = roll_rows(v_raw[...], twice, shift)
    v_out[...] = v.astype(jnp.bfloat16)
    v_t = v.T.astype(jnp.bfloat16)
    for first, count, key_first, key_count in query_spans(rows):
        block = q_out[first : first + count]
        pieces = []
        for head in range(2):
            scores = dot_rows(k_out[key_first : key_first + key_count], only_head(block, head))
            if key_first:
                scores = jnp.where(ids_col[...] == ids_row[...], scores, NEG_FILL)
            peak = jnp.max(fold_rows(jnp.maximum, scores), axis=0, keepdims=True)
            weights = jnp.exp(scores - peak)
            total = jnp.sum(fold_rows(jnp.add, weights), axis=0, keepdims=True)
            lse_out[0, head : head + 1, first : first + count] = peak + jnp.log(total)
            piece = dot_plain(
                v_t[head * DH : (head + 1) * DH, key_first : key_first + key_count],
                weights.astype(jnp.bfloat16),
            )
            pieces.append(piece / total)
        att_scr[first : first + count] = jnp.concatenate(pieces, axis=0).T
    back = lax.rem(rows - shift, rows)
    att_out[...] = roll_rows(att_scr[...], twice, back).astype(jnp.bfloat16)


def backward_kernel(
    shift_ref, q_ref, k_ref, v_ref, grad_ref, att_ref, lse_ref, cos_ref, sin_ref, ids_col, ids_row,
    dq_out, dk_out, dv_out, twice, grad_scr, inner_scr, key_t, dq_scr, dk_scr, dv_scr,
):
    rows = q_ref.shape[0]
    shift = shift_ref[0]
    grad = grad_ref[...].astype(jnp.float32)
    products = roll_rows(grad * att_ref[...].astype(jnp.float32), twice, shift).T
    inner_scr[0:1] = jnp.sum(products[:DH], axis=0, keepdims=True)
    inner_scr[1:2] = jnp.sum(products[DH:], axis=0, keepdims=True)
    grad_scr[...] = roll_rows(grad, twice, shift).astype(jnp.bfloat16)
    key_t[...] = k_ref[...].astype(jnp.float32).T.astype(jnp.bfloat16)
    for first, count, key_first, key_count in query_spans(rows):
        keys = slice(key_first, key_first + key_count)
        block = slice(first, first + count)
        pieces, probs_low, scores_low, queries_head, grads_head = [], [], [], [], []
        for head in range(2):
            q_head = only_head(q_ref[block], head)
            g_head = only_head(grad_scr[block], head)
            scores = dot_rows(k_ref[keys], q_head)
            probs = jnp.exp(scores - lse_ref[0, head : head + 1, block])
            if key_first:
                probs = jnp.where(ids_col[...] == ids_row[...], probs, 0.0)
            grad_probs = dot_rows(v_ref[keys], g_head)
            grad_scores = probs * (grad_probs - inner_scr[head : head + 1, block])
            grad_scores = grad_scores.astype(jnp.bfloat16)
            pieces.append(dot_plain(key_t[head * DH : (head + 1) * DH, keys], grad_scores))
            probs_low.append(probs.astype(jnp.bfloat16))
            scores_low.append(grad_scores)
            queries_head.append(q_head)
            grads_head.append(g_head)
        dv_part = dot_plain(
            jnp.concatenate(probs_low, axis=1), jnp.concatenate(grads_head, axis=0)
        )
        dk_part = dot_plain(
            jnp.concatenate(scores_low, axis=1), jnp.concatenate(queries_head, axis=0)
        )
        if first % LONG == 0:
            dv_scr[keys] = dv_part
            dk_scr[keys] = dk_part
        else:
            dv_scr[keys] = dv_scr[keys] + dv_part
            dk_scr[keys] = dk_scr[keys] + dk_part
        dq_scr[block] = jnp.concatenate(pieces, axis=0).T * 0.125
    back = lax.rem(rows - shift, rows)
    cos, sin = cos_ref[...], sin_ref[...]
    dq = roll_rows(dq_scr[...], twice, back)
    dq_out[...] = (dq * cos - turn_lanes(dq) * sin).astype(jnp.bfloat16)
    dk = roll_rows(dk_scr[...], twice, back)
    dk_out[...] = (dk * cos - turn_lanes(dk) * sin).astype(jnp.bfloat16)
    dv_out[...] = roll_rows(dv_scr[...], twice, back).astype(jnp.bfloat16)


def attention_forward(projected, tables, shift, rest_ids):
    rows = projected.shape[0]
    pairs = projected.shape[1] // (6 * DH)
    pair = (rows, 2 * DH)
    rest = rows - LONG
    flat = jax.ShapeDtypeStruct((rows, pairs * 2 * DH), jnp.bfloat16)
    spec = pl.BlockSpec(pair, lambda p, s: (0, p))
    whole = lambda shape: pl.BlockSpec(shape, lambda p, s: (0, 0))
    return pl.pallas_call(
        forward_kernel,
        grid_spec=pltpu.PrefetchScalarGridSpec(
            num_scalar_prefetch=1,
            grid=(pairs,),
            in_specs=[
                spec,
                pl.BlockSpec(pair, lambda p, s: (0, pairs + p)),
                pl.BlockSpec(pair, lambda p, s: (0, 2 * pairs + p)),
                whole(pair),
                whole(pair),
                whole((rest, 1)),
                whole((1, rest)),
            ],
            out_specs=[spec, spec, spec, spec, pl.BlockSpec((1, 2, rows), lambda p, s: (p, 0, 0))],
            scratch_shapes=[
                pltpu.VMEM((2 * rows, 2 * DH), jnp.float32),
                pltpu.VMEM(pair, jnp.float32),
            ],
        ),
        out_shape=[flat, flat, flat, flat, jax.ShapeDtypeStruct((pairs, 2, rows), jnp.float32)],
        compiler_params=pltpu.CompilerParams(vmem_limit_bytes=48 << 20),
        cost_estimate=cost(8e9 * pairs, 25e6 * pairs / 4, 3e6 * pairs),
        name="attention_forward",
    )(shift, projected, projected, projected, *tables, rest_ids[:, None], rest_ids[None, :])


def attention_backward(
    queries, keys, values, grads, attended, lse, tables, shift, rest_ids, first_pair, pairs
):
    rows = queries.shape[0]
    pair = (rows, 2 * DH)
    rest = rows - LONG
    flat = jax.ShapeDtypeStruct((rows, pairs * 2 * DH), jnp.bfloat16)
    spec = pl.BlockSpec(pair, lambda p, s: (0, first_pair + p))
    out_spec = pl.BlockSpec(pair, lambda p, s: (0, p))
    whole = lambda shape: pl.BlockSpec(shape, lambda p, s: (0, 0))
    return pl.pallas_call(
        backward_kernel,
        grid_spec=pltpu.PrefetchScalarGridSpec(
            num_scalar_prefetch=1,
            grid=(pairs,),
            in_specs=[
                spec,
                spec,
                spec,
                spec,
                spec,
                pl.BlockSpec((1, 2, rows), lambda p, s: (first_pair + p, 0, 0)),
                whole(pair),
                whole(pair),
                whole((rest, 1)),
                whole((1, rest)),
            ],
            out_specs=[out_spec, out_spec, out_spec],
            scratch_shapes=[
                pltpu.VMEM((2 * rows, 2 * DH), jnp.float32),
                pltpu.VMEM(pair, jnp.bfloat16),
                pltpu.VMEM((8, rows), jnp.float32),
                pltpu.VMEM((2 * DH, rows), jnp.bfloat16),
                pltpu.VMEM(pair, jnp.float32),
                pltpu.VMEM(pair, jnp.float32),
                pltpu.VMEM(pair, jnp.float32),
            ],
        ),
        out_shape=[flat, flat, flat],
        compiler_params=pltpu.CompilerParams(vmem_limit_bytes=48 << 20),
        cost_estimate=cost(8e9 * pairs, 25e6 * pairs / 4, 3e6 * pairs),
        name="attention_backward",
    )(shift, queries, keys, values, grads, attended, lse, *tables, rest_ids[:, None], rest_ids[None, :])


def norm_rows(values):
    center = values - jnp.mean(values, axis=-1, keepdims=True)
    scale_back = lax.rsqrt(jnp.mean(center * center, axis=-1, keepdims=True) + NORM_EPS)
    return center * scale_back, scale_back


def residual_rows(x_ref, own_ref, other_ref):
    total = own_ref[...].astype(jnp.float32) + other_ref[...].astype(jnp.float32)
    return x_ref[...].astype(jnp.float32) + total


def feedforward_kernel(
    x_ref, own_ref, other_ref, grad_ref, gain_ref, weights_ref,
    h_out, act_out, lift_out, grad_h_out, mlp_out,
):
    padded = act_out.shape[1]
    up_ref, down_ref = weights_ref.at[:, : 2 * padded], weights_ref.at[:, 2 * padded :]
    normed, _ = norm_rows(residual_rows(x_ref, own_ref, other_ref))
    hidden = (normed * gain_ref[...]).astype(jnp.bfloat16)
    h_out[...] = hidden
    gate = dot_plain(hidden, up_ref[:, :padded])
    value = dot_plain(hidden, up_ref[:, padded:])
    grad_act = dot_plain(grad_ref[...], down_ref[...])
    gelu_value, gelu_slope = gelu_pair(gate)
    act = (gelu_value * value).astype(jnp.bfloat16)
    act_out[...] = act
    mlp_out[...] = dot_rows(act, down_ref[...]).astype(jnp.bfloat16)
    lift_out[:, :padded] = (grad_act * value * gelu_slope).astype(jnp.bfloat16)
    lift_out[:, padded:] = (grad_act * gelu_value).astype(jnp.bfloat16)
    grad_h_out[...] = dot_rows(lift_out[...], up_ref[...]).astype(jnp.bfloat16)


def middle_kernel(
    x_ref, own_ref, other_ref, gh_own_ref, gh_other_ref, grad_ref, gain_ref, out_ref,
    resid_out, low_out, att_out, gain_out,
):
    normed, scale_back = norm_rows(residual_rows(x_ref, own_ref, other_ref))
    grad_h = gh_own_ref[...].astype(jnp.float32) + gh_other_ref[...].astype(jnp.float32)
    result = grad_ref[...].astype(jnp.float32) + norm_backward(
        grad_h, normed, scale_back, gain_ref[...]
    )
    resid_out[...] = result
    low = result.astype(jnp.bfloat16)
    low_out[...] = low
    att_out[...] = dot_plain(low, out_ref[...]).astype(jnp.bfloat16)

    @pl.when(pl.program_id(0) == 0)
    def _():
        gain_out[...] = jnp.zeros_like(gain_out)

    gain_out[...] = gain_out[...] + jnp.sum(grad_h * normed, axis=0, keepdims=True)


def first_hidden_kernel(x_ref, weights_ref, *refs):
    part_refs, (partial_out, gain_out) = refs[:-2], refs[-2:]
    normed, _ = norm_rows(x_ref[...].astype(jnp.float32))
    grads = jnp.concatenate([ref[...] for ref in part_refs], axis=1)
    partial = dot_rows(grads, weights_ref[...])
    partial_out[...] = partial.astype(jnp.bfloat16)

    @pl.when(pl.program_id(0) == 0)
    def _():
        gain_out[...] = jnp.zeros_like(gain_out)

    gain_out[...] = gain_out[...] + jnp.sum(partial * normed, axis=0, keepdims=True)


def first_hidden(x, weights, parts, first_row):
    rows, width = x.shape
    tile = row_tile(rows)
    skip = first_row // tile
    return pl.pallas_call(
        first_hidden_kernel,
        grid=(rows // tile,),
        in_specs=[pl.BlockSpec((tile, width), lambda i: (i, 0)), fixed_block(weights.shape)]
        + [pl.BlockSpec((tile, part.shape[1]), lambda i: (skip + i, 0)) for part in parts],
        out_specs=[
            pl.BlockSpec((tile, width), lambda i: (i, 0)),
            pl.BlockSpec((1, width), lambda i: (0, 0)),
        ],
        out_shape=[
            jax.ShapeDtypeStruct((rows, width), jnp.bfloat16),
            jax.ShapeDtypeStruct((1, width), jnp.float32),
        ],
        compiler_params=pltpu.CompilerParams(vmem_limit_bytes=48 << 20),
        cost_estimate=cost(6 * rows * width * width // 2, 10 * rows * width),
        name="first_hidden",
    )(x, weights, *parts)


def row_tile(rows):
    for tile in (320, 256, 160, 128, 64, 32, 16):
        if rows % tile == 0:
            return tile
    return rows


def fixed_block(shape):
    return pl.BlockSpec(shape, lambda i: (0, 0), pipeline_mode=pl.Buffered(1))


def feedforward(x, own, other, grads, gain, weights):
    rows, width = x.shape
    padded = weights.shape[1] // 3
    tile = row_tile(rows)
    spec = lambda columns: pl.BlockSpec((tile, columns), lambda i: (i, 0))
    out = lambda columns: jax.ShapeDtypeStruct((rows, columns), jnp.bfloat16)
    return pl.pallas_call(
        feedforward_kernel,
        grid=(rows // tile,),
        in_specs=[spec(width)] * 4
        + [fixed_block((1, width)), fixed_block(weights.shape)],
        out_specs=[spec(width), spec(padded), spec(2 * padded), spec(width), spec(width)],
        out_shape=[out(width), out(padded), out(2 * padded), out(width), out(width)],
        compiler_params=pltpu.CompilerParams(vmem_limit_bytes=56 << 20),
        cost_estimate=cost(12 * rows * width * padded, 16 * rows * width, 2 * rows * padded),
        name="feedforward",
    )(x, own, other, grads, gain[None, :], weights)


def middle(x, own, other, gh_own, gh_other, grads, gain, w_out_t):
    rows, width = x.shape
    columns = w_out_t.shape[1]
    tile = row_tile(rows)
    spec = lambda columns: pl.BlockSpec((tile, columns), lambda i: (i, 0))
    return pl.pallas_call(
        middle_kernel,
        grid=(rows // tile,),
        in_specs=[spec(width)] * 6 + [fixed_block((1, width)), fixed_block(w_out_t.shape)],
        out_specs=[
            spec(width),
            spec(width),
            spec(columns),
            pl.BlockSpec((1, width), lambda i: (0, 0)),
        ],
        out_shape=[
            jax.ShapeDtypeStruct((rows, width), jnp.float32),
            jax.ShapeDtypeStruct((rows, width), jnp.bfloat16),
            jax.ShapeDtypeStruct((rows, columns), jnp.bfloat16),
            jax.ShapeDtypeStruct((1, width), jnp.float32),
        ],
        compiler_params=pltpu.CompilerParams(vmem_limit_bytes=48 << 20),
        cost_estimate=cost(2 * rows * width * columns, 20 * rows * width),
        name="middle",
    )(x, own, other, gh_own, gh_other, grads, gain[None, :], w_out_t)


def swap_pairs(values):
    return lax.ppermute(values, "tensor", [(0, 1), (1, 0)])


def gather_rows(values):
    if lax.axis_size("tensor") == 2:
        return [values, swap_pairs(values)]
    rows = values.shape[0]
    every = lax.all_gather(values, "tensor", axis=0, tiled=True)
    index = lax.axis_index("tensor")
    own_first = jnp.roll(every, -index * rows, axis=0)
    return [own_first[:rows], own_first[rows:]]


def sum_over_tensor(own, other):
    if lax.axis_size("tensor") == 2:
        first = swap_pairs(other)
        own_late, first = lax.optimization_barrier((own, first))
        return [first, swap_pairs(own_late)]
    rows, index = own.shape[0], lax.axis_index("tensor")
    full = jnp.roll(jnp.concatenate([own, other], axis=0), index * rows, axis=0)
    full = lax.psum(full, "tensor")
    full = jnp.roll(full, -index * rows, axis=0)
    return [full[:rows] - own, full[rows:] - other]


def exchange_both(own, other):
    if lax.axis_size("tensor") == 2:
        first = swap_pairs(own)
        other_late, first = lax.optimization_barrier((other, first))
        return [swap_pairs(other_late), first]
    return sum_over_tensor(own, other)


def receive_own(own, other):
    if lax.axis_size("tensor") == 2:
        return swap_pairs(other)
    rows, index = own.shape[0], lax.axis_index("tensor")
    full = jnp.roll(jnp.concatenate([own, other], axis=0), index * rows, axis=0)
    total = lax.psum_scatter(full, "tensor", scatter_dimension=0, tiled=True)
    return total - own


def sum_everywhere(values):
    total = lax.axis_size("dp") * lax.axis_size("tensor")
    if total & (total - 1):
        return lax.psum(values, ("dp", "tensor"))
    step = 1
    while step < total:
        pairs = [(i, i ^ step) for i in range(total)]
        values = values + lax.ppermute(values, ("dp", "tensor"), pairs)
        step *= 2
    return values


def gather_weights(shard):
    return lax.all_gather(shard, "dp", axis=0, tiled=True)


def exchange_bit(values, bit):
    size = lax.axis_size("dp")
    return lax.ppermute(values, "dp", [(i, i ^ bit) for i in range(size)])


def gather_doubling(shard):
    size, index = lax.axis_size("dp"), lax.axis_index("dp")
    if size & (size - 1):
        return gather_weights(shard)
    rows, columns = shard.shape
    state, bit = shard[None], size // 2
    while bit:
        received = exchange_bit(state, bit)
        high = (index // bit) % 2 == 1
        both = [jnp.where(high, received, state), jnp.where(high, state, received)]
        state = jnp.stack(both, axis=1).reshape(-1, rows, columns)
        bit //= 2
    return state.reshape(size * rows, columns)


def scatter_halving(full):
    size, index = lax.axis_size("dp"), lax.axis_index("dp")
    if size & (size - 1):
        return scatter_sums(full).astype(jnp.float32)
    rows, columns = full.shape[0] // size, full.shape[1]
    state, bit = full, 1
    while bit < size:
        halves = state.astype(jnp.bfloat16).reshape(-1, 2, rows, columns)
        mine = (index // bit) % 2
        received = exchange_bit(
            lax.dynamic_index_in_dim(halves, 1 - mine, axis=1, keepdims=False), bit
        )
        kept = lax.dynamic_index_in_dim(halves, mine, axis=1, keepdims=False)
        state = kept.astype(jnp.float32) + received.astype(jnp.float32)
        bit *= 2
    return state.reshape(rows, columns)


def scatter_sums(full):
    return lax.psum_scatter(full, "dp", scatter_dimension=0, tiled=True)


def matmul_low(equation, left, right):
    product = jnp.einsum(equation, left, right, preferred_element_type=jnp.float32)
    return product.astype(jnp.bfloat16)


def local(
    tokens,
    lengths,
    attention_norm1_gain,
    qkv_weight,
    out_weight,
    feedforward_norm2_gain,
    up_weight,
    down_weight,
    output_gradient,
):
    own_rows = tokens.shape[0]
    group_rows = own_rows * lax.axis_size("tensor")
    shard_rows, width = qkv_weight.shape[0], qkv_weight.shape[2]
    hidden = up_weight.shape[2]
    padded = -(-hidden // 128) * 128
    w_qkv = gather_weights(qkv_weight.reshape(shard_rows, 3 * width))
    up_shard = jnp.pad(up_weight, ((0, 0), (0, 0), (0, padded - hidden)))
    down_shard = jnp.pad(down_weight.T, ((0, 0), (0, padded - hidden)))
    w_ffn = gather_weights(
        jnp.concatenate([up_shard.reshape(shard_rows, 2 * padded), down_shard], axis=1)
    )
    w_out_t = gather_doubling(out_weight.T)

    first_place = lax.axis_index("tensor") * own_rows
    places = (jnp.arange(group_rows, dtype=jnp.int32) + first_place) % group_rows
    tables = rope_tables(lengths[0], places)
    long_start = jnp.sum(
        jnp.where(lengths[0] == LONG, jnp.cumsum(lengths[0]) - lengths[0], 0)
    ).astype(jnp.int32)
    shift = ((long_start - first_place) % group_rows).astype(jnp.int32).reshape(1)
    rest_places = (long_start + jnp.arange(LONG, group_rows, dtype=jnp.int32)) % group_rows
    rest_ids = sequence_ids(lengths[0], rest_places)

    token_parts = gather_rows(tokens)
    normed = [apply_norm(part.astype(jnp.float32)) for part in token_parts]
    h_one_all = jnp.concatenate(
        [(values * attention_norm1_gain).astype(jnp.bfloat16) for values, _ in normed], axis=0
    )
    projected = jnp.dot(h_one_all, w_qkv, preferred_element_type=jnp.float32)
    queries, keys, values, attended, lse = attention_forward(projected, tables, shift, rest_ids)
    late_gradient, _ = lax.optimization_barrier((output_gradient, token_parts[1]))
    grad_parts = gather_rows(late_gradient)
    attended, grad_parts[1] = lax.optimization_barrier((attended, grad_parts[1]))

    attn_other = matmul_low("th,dh->td", attended[own_rows:], w_out_t)
    attn_own = matmul_low("th,dh->td", attended[:own_rows], w_out_t)
    own_parts = [attn_own, attn_other]
    received = sum_over_tensor(attn_own, attn_other)

    def feed(index):
        return feedforward(
            token_parts[index],
            own_parts[index],
            received[index],
            grad_parts[index],
            feedforward_norm2_gain,
            w_ffn,
        )

    fed = [feed(0), feed(1)]
    h_two, act, grad_lift, grad_h2, mlp = [list(pair) for pair in zip(*fed)]
    gh_received = exchange_both(grad_h2[0], grad_h2[1])
    join = lambda pair: jnp.concatenate(pair, axis=0)
    grad_rows_all = join(grad_parts)
    grad_down_full = matmul_low("td,tf->df", grad_rows_all, join(act))
    grad_up_full = matmul_low("td,th->dh", join(h_two), join(grad_lift))
    ffn_sums = jnp.concatenate([grad_up_full, grad_down_full], axis=1)
    ffn_sums, gh_received[1] = lax.optimization_barrier((ffn_sums, gh_received[1]))
    ffn_part = scatter_sums(ffn_sums)

    mids = [
        middle(
            token_parts[index],
            own_parts[index],
            received[index],
            grad_h2[index],
            gh_received[index],
            grad_parts[index],
            feedforward_norm2_gain,
            w_out_t,
        )
        for index in range(2)
    ]
    residual_gradient, gain_gradient_second = mids[0][0], mids[0][3][0]
    grad_resid_all = join([mids[0][1], mids[1][1]])
    grad_attended = join([mids[0][2], mids[1][2]])
    mlp[1] = lax.optimization_barrier((mlp[1], gh_received[1]))[0]
    mlp_received = receive_own(mlp[0], mlp[1])

    pairs = width // (2 * DH)
    calls = 2 if pairs % 2 == 0 else 1
    grad_pieces, sums = [], []
    for call in range(calls):
        piece = attention_backward(
            queries,
            keys,
            values,
            grad_attended,
            attended,
            lse,
            tables,
            shift,
            rest_ids,
            call * (pairs // calls),
            pairs // calls,
        )
        grad_pieces.append(piece)
        columns = matmul_low("td,tc->dc", h_one_all, jnp.concatenate(piece, axis=1))
        if call == 0:
            grad_out_full = matmul_low("td,th->dh", grad_resid_all, attended)
            columns = jnp.concatenate([columns, grad_out_full], axis=1)
        sums.append(scatter_halving(columns))

    parts = [grad_pieces[call][which] for which in range(3) for call in range(calls)]
    grad_h1_other, gain_other = first_hidden(token_parts[1], w_qkv, parts, own_rows)
    grad_h1_own, gain_own = first_hidden(token_parts[0], w_qkv, parts, 0)
    first_hidden_gradient = grad_h1_own.astype(jnp.float32) + receive_own(
        grad_h1_own, grad_h1_other
    ).astype(jnp.float32)
    gain_grads = sum_everywhere(
        jnp.concatenate([gain_own + gain_other, gain_gradient_second[None]], axis=0)
    )
    mixed = (
        tokens.astype(jnp.float32)
        + (attn_own.astype(jnp.float32) + received[0].astype(jnp.float32))
        + (mlp[0].astype(jnp.float32) + mlp_received.astype(jnp.float32))
    ).astype(jnp.bfloat16)
    own_scaled1, inverse_deviation1 = normed[0]
    token_gradients = residual_gradient + norm_backward(
        first_hidden_gradient, own_scaled1, inverse_deviation1, attention_norm1_gain
    )
    ffn_part = ffn_part.astype(jnp.float32)
    qkv_part = jnp.concatenate(
        [
            part[:, : 3 * width // calls].reshape(shard_rows, 3, width // calls)
            for part in sums
        ],
        axis=2,
    )
    return (
        mixed,
        token_gradients,
        gain_grads[0],
        qkv_part,
        sums[0][:, 3 * width // calls :].T,
        gain_grads[1],
        ffn_part[:, : 2 * padded].reshape(shard_rows, 2, padded)[:, :, :hidden],
        ffn_part[:, 2 * padded : 2 * padded + hidden].T,
    )


def solution(mesh):
    return jax.shard_map(
        local,
        mesh=mesh,
        in_specs=(
            P(("dp", "tensor"), None),
            P("dp", None),
            P(),
            P("dp", None, "tensor"),
            P("tensor", "dp"),
            P(),
            P("dp", None, "tensor"),
            P("tensor", "dp"),
            P(("dp", "tensor"), None),
        ),
        out_specs=(
            P(("dp", "tensor"), None),
            P(("dp", "tensor"), None),
            P(),
            P("dp", None, "tensor"),
            P("tensor", "dp"),
            P(),
            P("dp", None, "tensor"),
            P("tensor", "dp"),
        ),
        check_vma=False,
    )
```

```python
import jax
import jax.numpy as jnp
from jax import lax
from jax.experimental import pallas as pl
from jax.experimental.pallas import tpu as pltpu
from jax.sharding import PartitionSpec as P


DH = 64


ROPE_BASE = 160000.0
NORM_EPS = 1e-05
NEG_FILL = -1e30


def sequence_ids(lengths_row, places):
    ends = jnp.cumsum(lengths_row)
    return jnp.sum((places[:, None] >= ends[None, :]).astype(jnp.int32), axis=1)


def rope_tables(lengths_row, places):
    ends = jnp.cumsum(lengths_row)
    segment_ids = sequence_ids(lengths_row, places)
    starts = ends - lengths_row
    member = segment_ids[:, None] == jnp.arange(lengths_row.shape[0], dtype=jnp.int32)[None, :]
    firsts = jnp.sum(jnp.where(member, starts[None, :], 0), axis=1)
    offsets = (places - firsts).astype(jnp.float32)
    freqs = ROPE_BASE ** (-jnp.arange(0, DH, 2).astype(jnp.float32) / DH)
    angles = offsets[:, None] * freqs[None, :]
    cosine, sine = jnp.cos(angles), jnp.sin(angles)
    return (
        jnp.concatenate([cosine, cosine, cosine, cosine], axis=1),
        jnp.concatenate([-sine, sine, -sine, sine], axis=1),
    )


def apply_norm(values):
    center = values - jnp.mean(values, axis=-1, keepdims=True)
    scale_back = lax.rsqrt(jnp.mean(center * center, axis=-1, keepdims=True) + NORM_EPS)
    return (center * scale_back, scale_back)


def norm_backward(grad_norm, normed, scale_back, gain):
    grad_hat = grad_norm * gain
    return scale_back * (
        grad_hat
        - jnp.mean(grad_hat, axis=-1, keepdims=True)
        - normed * jnp.mean(grad_hat * normed, axis=-1, keepdims=True)
    )


def gelu_pair(values):
    cdf = 0.5 * (1.0 + jax.scipy.special.erf(values * 0.7071067811865476))
    density = jnp.exp(-0.5 * values * values) * 0.3989422804014327
    return (values * cdf, cdf + values * density)


LONG = 1024
QUERY_BLOCK = 512


def head_lanes(rows):
    return lax.broadcasted_iota(jnp.int32, (rows, 2 * DH), 1)


def turn_lanes(values):
    lanes = head_lanes(values.shape[0]) % DH
    return jnp.where(
        lanes < DH // 2,
        pltpu.roll(values, 2 * DH - DH // 2, 1),
        pltpu.roll(values, DH // 2, 1),
    )


def roll_rows(values, twice_ref, first):
    rows = values.shape[0]
    twice_ref[:rows] = values
    twice_ref[rows:] = values
    return twice_ref[pl.ds(first, rows), :]


def only_head(values, head):
    lanes = head_lanes(values.shape[0])
    return jnp.where((lanes >= head * DH) & (lanes < (head + 1) * DH), values, 0)


def dot_rows(left, right):
    return lax.dot_general(
        left, right, (((1,), (1,)), ((), ())), preferred_element_type=jnp.float32
    )


def dot_plain(left, right):
    return lax.dot_general(
        left, right, (((1,), (0,)), ((), ())), preferred_element_type=jnp.float32
    )


def cost(flops, bytes_accessed, transcendentals=0):
    return pl.CostEstimate(
        flops=int(flops), bytes_accessed=int(bytes_accessed), transcendentals=int(transcendentals)
    )


def query_spans(rows):
    spans = [(first, QUERY_BLOCK, 0, LONG) for first in range(0, LONG, QUERY_BLOCK)]
    return spans + [(LONG, rows - LONG, LONG, rows - LONG)]


def forward_kernel(
    shift_ref, q_raw, k_raw, v_raw, cos_ref, sin_ref, ids_col, ids_row,
    q_out, k_out, v_out, att_out, lse_out, twice, att_scr,
):
    rows = q_raw.shape[0]
    shift = shift_ref[0]
    cos, sin = cos_ref[...], sin_ref[...]
    q = q_raw[...]
    q = roll_rows(q * cos + turn_lanes(q) * sin, twice, shift).astype(jnp.bfloat16) * 0.125
    q_out[...] = q.astype(jnp.bfloat16)
    k = k_raw[...]
    k_out[...] = roll_rows(k * cos + turn_lanes(k) * sin, twice, shift).astype(jnp.bfloat16)
    v_out[...] = roll_rows(v_raw[...], twice, shift).astype(jnp.bfloat16)
    for first, count, key_first, key_count in query_spans(rows):
        block = q_out[first : first + count]
        keys = slice(key_first, key_first + key_count)
        both, logs = [], []
        for head in range(2):
            scores = dot_rows(only_head(block, head), k_out[keys])
            if key_first:
                scores = jnp.where(ids_col[...] == ids_row[...], scores, NEG_FILL)
            peak = jnp.max(scores, axis=1, keepdims=True)
            weights = jnp.exp(scores - peak)
            total = jnp.sum(weights, axis=1, keepdims=True)
            logs.append(jnp.broadcast_to(peak + jnp.log(total), (count, 2 * DH)))
            both.append(dot_plain(weights.astype(jnp.bfloat16), v_out[keys]) * (1.0 / total))
        low_head = head_lanes(count) < DH
        att_scr[first : first + count] = jnp.where(low_head, both[0], both[1])
        logs = jnp.where(low_head, logs[0], logs[1]).T
        lse_out[0, 0:1, first : first + count] = logs[0:1]
        lse_out[0, 1:2, first : first + count] = logs[DH : DH + 1]
    back = lax.rem(rows - shift, rows)
    att_out[...] = roll_rows(att_scr[...], twice, back).astype(jnp.bfloat16)


def backward_kernel(
    shift_ref, q_ref, k_ref, v_ref, grad_ref, att_ref, lse_ref, cos_ref, sin_ref, ids_col, ids_row,
    dq_out, dk_out, dv_out, twice, grad_scr, inner_scr, key_t, dq_scr, dk_scr, dv_scr,
):
    rows = q_ref.shape[0]
    shift = shift_ref[0]
    grad = grad_ref[...].astype(jnp.float32)
    products = roll_rows(grad * att_ref[...].astype(jnp.float32), twice, shift).T
    inner_scr[0:1] = jnp.sum(products[:DH], axis=0, keepdims=True)
    inner_scr[1:2] = jnp.sum(products[DH:], axis=0, keepdims=True)
    grad_scr[...] = roll_rows(grad, twice, shift).astype(jnp.bfloat16)
    key_t[...] = k_ref[...].astype(jnp.float32).T.astype(jnp.bfloat16)
    for first, count, key_first, key_count in query_spans(rows):
        keys = slice(key_first, key_first + key_count)
        block = slice(first, first + count)
        pieces, probs_low, scores_low, queries_head, grads_head = [], [], [], [], []
        for head in range(2):
            q_head = only_head(q_ref[block], head)
            g_head = only_head(grad_scr[block], head)
            scores = dot_rows(k_ref[keys], q_head)
            probs = jnp.exp(scores - lse_ref[0, head : head + 1, block])
            if key_first:
                probs = jnp.where(ids_col[...] == ids_row[...], probs, 0.0)
            grad_probs = dot_rows(v_ref[keys], g_head)
            grad_scores = probs * (grad_probs - inner_scr[head : head + 1, block])
            grad_scores = grad_scores.astype(jnp.bfloat16)
            pieces.append(dot_plain(key_t[head * DH : (head + 1) * DH, keys], grad_scores))
            probs_low.append(probs.astype(jnp.bfloat16))
            scores_low.append(grad_scores)
            queries_head.append(q_head)
            grads_head.append(g_head)
        dv_part = dot_plain(
            jnp.concatenate(probs_low, axis=1), jnp.concatenate(grads_head, axis=0)
        )
        dk_part = dot_plain(
            jnp.concatenate(scores_low, axis=1), jnp.concatenate(queries_head, axis=0)
        )
        if first % LONG == 0:
            dv_scr[keys] = dv_part
            dk_scr[keys] = dk_part
        else:
            dv_scr[keys] = dv_scr[keys] + dv_part
            dk_scr[keys] = dk_scr[keys] + dk_part
        dq_scr[block] = jnp.concatenate(pieces, axis=0).T * 0.125
    back = lax.rem(rows - shift, rows)
    cos, sin = cos_ref[...], sin_ref[...]
    dq = roll_rows(dq_scr[...], twice, back)
    dq_out[...] = (dq * cos - turn_lanes(dq) * sin).astype(jnp.bfloat16)
    dk = roll_rows(dk_scr[...], twice, back)
    dk_out[...] = (dk * cos - turn_lanes(dk) * sin).astype(jnp.bfloat16)
    dv_out[...] = roll_rows(dv_scr[...], twice, back).astype(jnp.bfloat16)


def attention_forward(projected, tables, shift, rest_ids):
    rows = projected.shape[0]
    pairs = projected.shape[1] // (6 * DH)
    pair = (rows, 2 * DH)
    rest = rows - LONG
    flat = jax.ShapeDtypeStruct((rows, pairs * 2 * DH), jnp.bfloat16)
    spec = pl.BlockSpec(pair, lambda p, s: (0, p))
    whole = lambda shape: pl.BlockSpec(shape, lambda p, s: (0, 0))
    return pl.pallas_call(
        forward_kernel,
        grid_spec=pltpu.PrefetchScalarGridSpec(
            num_scalar_prefetch=1,
            grid=(pairs,),
            in_specs=[
                spec,
                pl.BlockSpec(pair, lambda p, s: (0, pairs + p)),
                pl.BlockSpec(pair, lambda p, s: (0, 2 * pairs + p)),
                whole(pair),
                whole(pair),
                whole((rest, 1)),
                whole((1, rest)),
            ],
            out_specs=[spec, spec, spec, spec, pl.BlockSpec((1, 2, rows), lambda p, s: (p, 0, 0))],
            scratch_shapes=[
                pltpu.VMEM((2 * rows, 2 * DH), jnp.float32),
                pltpu.VMEM(pair, jnp.float32),
            ],
        ),
        out_shape=[flat, flat, flat, flat, jax.ShapeDtypeStruct((pairs, 2, rows), jnp.float32)],
        compiler_params=pltpu.CompilerParams(vmem_limit_bytes=48 << 20),
        cost_estimate=cost(8e9 * pairs, 25e6 * pairs / 4, 3e6 * pairs),
        name="attention_forward",
    )(shift, projected, projected, projected, *tables, rest_ids[:, None], rest_ids[None, :])


def attention_backward(
    queries, keys, values, grads, attended, lse, tables, shift, rest_ids, first_pair, pairs
):
    rows = queries.shape[0]
    pair = (rows, 2 * DH)
    rest = rows - LONG
    flat = jax.ShapeDtypeStruct((rows, pairs * 2 * DH), jnp.bfloat16)
    spec = pl.BlockSpec(pair, lambda p, s: (0, first_pair + p))
    out_spec = pl.BlockSpec(pair, lambda p, s: (0, p))
    whole = lambda shape: pl.BlockSpec(shape, lambda p, s: (0, 0))
    return pl.pallas_call(
        backward_kernel,
        grid_spec=pltpu.PrefetchScalarGridSpec(
            num_scalar_prefetch=1,
            grid=(pairs,),
            in_specs=[
                spec,
                spec,
                spec,
                spec,
                spec,
                pl.BlockSpec((1, 2, rows), lambda p, s: (first_pair + p, 0, 0)),
                whole(pair),
                whole(pair),
                whole((rest, 1)),
                whole((1, rest)),
            ],
            out_specs=[out_spec, out_spec, out_spec],
            scratch_shapes=[
                pltpu.VMEM((2 * rows, 2 * DH), jnp.float32),
                pltpu.VMEM(pair, jnp.bfloat16),
                pltpu.VMEM((8, rows), jnp.float32),
                pltpu.VMEM((2 * DH, rows), jnp.bfloat16),
                pltpu.VMEM(pair, jnp.float32),
                pltpu.VMEM(pair, jnp.float32),
                pltpu.VMEM(pair, jnp.float32),
            ],
        ),
        out_shape=[flat, flat, flat],
        compiler_params=pltpu.CompilerParams(vmem_limit_bytes=48 << 20),
        cost_estimate=cost(8e9 * pairs, 25e6 * pairs / 4, 3e6 * pairs),
        name="attention_backward",
    )(shift, queries, keys, values, grads, attended, lse, *tables, rest_ids[:, None], rest_ids[None, :])


def norm_rows(values):
    center = values - jnp.mean(values, axis=-1, keepdims=True)
    scale_back = lax.rsqrt(jnp.mean(center * center, axis=-1, keepdims=True) + NORM_EPS)
    return center * scale_back, scale_back


def feedforward_kernel(
    x_ref, att_own_ref, att_other_ref, grad_ref, gain_ref, weights_ref, mix_ref,
    resid_out, h_out, act_out, lift_out, grad_h_out, mlp_out,
):
    padded = act_out.shape[1]
    width = att_own_ref.shape[1]
    resid = x_ref[...].astype(jnp.float32) + dot_rows(att_own_ref[...], mix_ref[:, :width])
    resid = resid + dot_rows(att_other_ref[...], mix_ref[:, width:])
    resid_out[...] = resid
    normed, _ = norm_rows(resid)
    hidden = (normed * gain_ref[...]).astype(jnp.bfloat16)
    h_out[...] = hidden
    gate = dot_plain(hidden, weights_ref[:, :padded])
    value = dot_plain(hidden, weights_ref[:, padded : 2 * padded])
    grad_act = dot_plain(grad_ref[...], weights_ref[:, 2 * padded :])
    gelu_value, gelu_slope = gelu_pair(gate)
    act = (gelu_value * value).astype(jnp.bfloat16)
    act_out[...] = act
    mlp_out[...] = dot_rows(act, weights_ref[:, 2 * padded :]).astype(jnp.bfloat16)
    lift_out[:, :padded] = (grad_act * value * gelu_slope).astype(jnp.bfloat16)
    lift_out[:, padded:] = (grad_act * gelu_value).astype(jnp.bfloat16)
    grad_h_out[...] = dot_rows(lift_out[...], weights_ref[:, : 2 * padded]).astype(jnp.bfloat16)


def middle_kernel(
    x_ref, gh_own_ref, gh_other_ref, grad_ref, gain_ref, out_ref,
    resid_out, low_out, att_own_out, att_other_out, gain_out,
):
    width = att_own_out.shape[1]
    normed, scale_back = norm_rows(x_ref[...])
    grad_h = gh_own_ref[...].astype(jnp.float32) + gh_other_ref[...].astype(jnp.float32)
    result = grad_ref[...].astype(jnp.float32) + norm_backward(
        grad_h, normed, scale_back, gain_ref[...]
    )
    resid_out[...] = result
    low = result.astype(jnp.bfloat16)
    low_out[...] = low
    att_own_out[...] = dot_plain(low, out_ref[:, :width]).astype(jnp.bfloat16)
    att_other_out[...] = dot_plain(low, out_ref[:, width:]).astype(jnp.bfloat16)

    @pl.when(pl.program_id(0) == 0)
    def _():
        gain_out[...] = jnp.zeros_like(gain_out)

    gain_out[...] = gain_out[...] + jnp.sum(grad_h * normed, axis=0, keepdims=True)


def first_hidden_kernel(x_ref, weights_ref, *refs):
    part_refs, (partial_out, gain_out) = refs[:-2], refs[-2:]
    normed, _ = norm_rows(x_ref[...].astype(jnp.float32))
    grads = jnp.concatenate([ref[...] for ref in part_refs], axis=1)
    partial = dot_rows(grads, weights_ref[...])
    partial_out[...] = partial.astype(jnp.bfloat16)

    @pl.when(pl.program_id(0) == 0)
    def _():
        gain_out[...] = jnp.zeros_like(gain_out)

    gain_out[...] = gain_out[...] + jnp.sum(partial * normed, axis=0, keepdims=True)


def first_hidden(x, weights, parts, first_row):
    rows, width = x.shape
    tile = row_tile(rows)
    skip = first_row // tile
    return pl.pallas_call(
        first_hidden_kernel,
        grid=(rows // tile,),
        in_specs=[pl.BlockSpec((tile, width), lambda i: (i, 0)), fixed_block(weights.shape)]
        + [pl.BlockSpec((tile, part.shape[1]), lambda i: (skip + i, 0)) for part in parts],
        out_specs=[
            pl.BlockSpec((tile, width), lambda i: (i, 0)),
            pl.BlockSpec((1, width), lambda i: (0, 0)),
        ],
        out_shape=[
            jax.ShapeDtypeStruct((rows, width), jnp.bfloat16),
            jax.ShapeDtypeStruct((1, width), jnp.float32),
        ],
        compiler_params=pltpu.CompilerParams(vmem_limit_bytes=48 << 20),
        cost_estimate=cost(6 * rows * width * width // 2, 10 * rows * width),
        name="first_hidden",
    )(x, weights, *parts)


def row_tile(rows):
    for tile in (320, 256, 160, 128, 64, 32, 16):
        if rows % tile == 0:
            return tile
    return rows


def fixed_block(shape):
    return pl.BlockSpec(shape, lambda i: (0, 0), pipeline_mode=pl.Buffered(1))


def feedforward(x, att_own, att_other, grads, gain, weights, mixers):
    rows, width = x.shape
    padded = weights.shape[1] // 3
    tile = row_tile(rows)
    spec = lambda columns: pl.BlockSpec((tile, columns), lambda i: (i, 0))
    out = lambda columns: jax.ShapeDtypeStruct((rows, columns), jnp.bfloat16)
    return pl.pallas_call(
        feedforward_kernel,
        grid=(rows // tile,),
        in_specs=[spec(width), spec(att_own.shape[1]), spec(att_other.shape[1]), spec(width)]
        + [fixed_block((1, width)), fixed_block(weights.shape), fixed_block(mixers.shape)],
        out_specs=[
            spec(width), spec(width), spec(padded), spec(2 * padded), spec(width), spec(width)
        ],
        out_shape=[
            jax.ShapeDtypeStruct((rows, width), jnp.float32),
            out(width),
            out(padded),
            out(2 * padded),
            out(width),
            out(width),
        ],
        compiler_params=pltpu.CompilerParams(vmem_limit_bytes=58 << 20),
        cost_estimate=cost(12 * rows * width * padded, 16 * rows * width, 2 * rows * padded),
        name="feedforward",
    )(x, att_own, att_other, grads, gain[None, :], weights, mixers)


def middle(x, gh_own, gh_other, grads, gain, mixers, own_columns, columns):
    rows, width = x.shape
    tile = row_tile(rows)
    spec = lambda columns: pl.BlockSpec((tile, columns), lambda i: (i, 0))
    low = lambda columns: jax.ShapeDtypeStruct((rows, columns), jnp.bfloat16)
    return pl.pallas_call(
        middle_kernel,
        grid=(rows // tile,),
        in_specs=[spec(width)] * 4 + [fixed_block((1, width)), fixed_block((width, columns))],
        out_specs=[
            spec(width),
            spec(width),
            spec(own_columns),
            spec(columns - own_columns),
            pl.BlockSpec((1, width), lambda i: (0, 0)),
        ],
        out_shape=[
            jax.ShapeDtypeStruct((rows, width), jnp.float32),
            low(width),
            low(own_columns),
            low(columns - own_columns),
            jax.ShapeDtypeStruct((1, width), jnp.float32),
        ],
        compiler_params=pltpu.CompilerParams(vmem_limit_bytes=48 << 20),
        cost_estimate=cost(2 * rows * width * columns, 20 * rows * width),
        name="middle",
    )(x, gh_own, gh_other, grads, gain[None, :], mixers)


def swap_pairs(values):
    return lax.ppermute(values, "tensor", [(0, 1), (1, 0)])


def gather_rows(values):
    if lax.axis_size("tensor") == 2:
        return [values, swap_pairs(values)]
    rows = values.shape[0]
    every = lax.all_gather(values, "tensor", axis=0, tiled=True)
    index = lax.axis_index("tensor")
    own_first = jnp.roll(every, -index * rows, axis=0)
    return [own_first[:rows], own_first[rows:]]


def gather_columns(values):
    width, index = values.shape[1], lax.axis_index("tensor")
    if lax.axis_size("tensor") == 2:
        return jnp.concatenate([values, swap_pairs(values)], axis=1)
    every = lax.all_gather(values, "tensor", axis=1, tiled=True)
    return jnp.roll(every, -index * width, axis=1)


def other_heads(attended, own_rows):
    if lax.axis_size("tensor") == 2:
        first = swap_pairs(attended[:own_rows])
        late, first = lax.optimization_barrier((attended[own_rows:], first))
        return [swap_pairs(late), first]
    shift = lax.axis_index("tensor") * own_rows
    every = gather_columns(jnp.roll(attended, shift, axis=0))
    every = jnp.roll(every, -shift, axis=0)[:, attended.shape[1] :]
    return [every[:own_rows], every[own_rows:]]


def collect_heads(sums, width):
    if lax.axis_size("tensor") == 2:
        low = sums[:, width:].astype(jnp.bfloat16)
        return sums[:, :width] + swap_pairs(low).astype(jnp.float32)
    index = lax.axis_index("tensor")
    natural = jnp.roll(sums, index * width, axis=1)
    return lax.dynamic_slice_in_dim(lax.psum(natural, "tensor"), index * width, width, axis=1)


def receive_own(own, other):
    if lax.axis_size("tensor") == 2:
        return swap_pairs(other)
    rows, index = own.shape[0], lax.axis_index("tensor")
    full = jnp.roll(jnp.concatenate([own, other], axis=0), index * rows, axis=0)
    total = lax.psum_scatter(full, "tensor", scatter_dimension=0, tiled=True)
    return total - own


def sum_everywhere(values):
    across = lax.axis_size("tensor")
    total = lax.axis_size("dp") * across
    if total & (total - 1):
        return lax.psum(values, ("dp", "tensor"))
    steps = [1 << power for power in range(total.bit_length() - 1)]
    for step in [s for s in steps if s >= across] + [s for s in steps if s < across]:
        pairs = [(i, i ^ step) for i in range(total)]
        values = values + lax.ppermute(values, ("dp", "tensor"), pairs)
    return values


def gather_weights(shard):
    return lax.all_gather(shard, "dp", axis=0, tiled=True)


def exchange_bit(values, bit):
    size = lax.axis_size("dp")
    return lax.ppermute(values, "dp", [(i, i ^ bit) for i in range(size)])


def gather_doubling(shard):
    size, index = lax.axis_size("dp"), lax.axis_index("dp")
    if size & (size - 1):
        return gather_weights(shard)
    rows, columns = shard.shape
    state, bit = shard[None], size // 2
    while bit:
        received = exchange_bit(state, bit)
        high = (index // bit) % 2 == 1
        both = [jnp.where(high, received, state), jnp.where(high, state, received)]
        state = jnp.stack(both, axis=1).reshape(-1, rows, columns)
        bit //= 2
    return state.reshape(size * rows, columns)


def scatter_halving(pieces):
    size, index = lax.axis_size("dp"), lax.axis_index("dp")
    if size & (size - 1):
        return scatter_sums(jnp.concatenate(pieces, axis=1)).astype(jnp.float32)
    rows, bit = pieces[0].shape[0] // size, 1

    def take(half):
        halves = [piece.reshape(-1, 2, rows, piece.shape[-1]) for piece in pieces]
        chosen = [
            lax.dynamic_index_in_dim(values, half, axis=1, keepdims=False) for values in halves
        ]
        return chosen[0] if len(chosen) == 1 else jnp.concatenate(chosen, axis=-1)

    while bit < size:
        mine = (index // bit) % 2
        received = exchange_bit(take(1 - mine).astype(jnp.bfloat16), bit)
        state = take(mine).astype(jnp.float32) + received.astype(jnp.float32)
        pieces = [state.astype(jnp.bfloat16)]
        bit *= 2
    return state.reshape(rows, -1)


def scatter_sums(full):
    return lax.psum_scatter(full, "dp", scatter_dimension=0, tiled=True)


def matmul_low(equation, left, right):
    product = jnp.einsum(equation, left, right, preferred_element_type=jnp.float32)
    return product.astype(jnp.bfloat16)


def local(
    tokens,
    lengths,
    attention_norm1_gain,
    qkv_weight,
    out_weight,
    feedforward_norm2_gain,
    up_weight,
    down_weight,
    output_gradient,
):
    own_rows = tokens.shape[0]
    group_rows = own_rows * lax.axis_size("tensor")
    shard_rows, width = qkv_weight.shape[0], qkv_weight.shape[2]
    hidden = up_weight.shape[2]
    padded = -(-hidden // 128) * 128
    w_qkv = gather_weights(qkv_weight.reshape(shard_rows, 3 * width))
    up_shard = jnp.pad(up_weight, ((0, 0), (0, 0), (0, padded - hidden)))
    down_shard = jnp.pad(down_weight.T, ((0, 0), (0, padded - hidden)))
    w_ffn = gather_weights(
        jnp.concatenate([up_shard.reshape(shard_rows, 2 * padded), down_shard], axis=1)
    )
    mixers = gather_columns(gather_doubling(out_weight.T))
    heads_width = mixers.shape[1]

    first_place = lax.axis_index("tensor") * own_rows
    places = (jnp.arange(group_rows, dtype=jnp.int32) + first_place) % group_rows
    tables = rope_tables(lengths[0], places)
    long_start = jnp.sum(
        jnp.where(lengths[0] == LONG, jnp.cumsum(lengths[0]) - lengths[0], 0)
    ).astype(jnp.int32)
    shift = ((long_start - first_place) % group_rows).astype(jnp.int32).reshape(1)
    rest_places = (long_start + jnp.arange(LONG, group_rows, dtype=jnp.int32)) % group_rows
    rest_ids = sequence_ids(lengths[0], rest_places)

    token_parts = gather_rows(tokens)
    normed = [apply_norm(part.astype(jnp.float32)) for part in token_parts]
    h_one_all = jnp.concatenate(
        [(values * attention_norm1_gain).astype(jnp.bfloat16) for values, _ in normed], axis=0
    )
    projected = jnp.dot(h_one_all, w_qkv, preferred_element_type=jnp.float32)
    queries, keys, values, attended, lse = attention_forward(projected, tables, shift, rest_ids)
    late_gradient, _ = lax.optimization_barrier((output_gradient, token_parts[1]))
    grad_parts = gather_rows(late_gradient)

    heads_received = other_heads(attended, own_rows)

    def feed(index):
        rows = slice(own_rows, None) if index else slice(own_rows)
        return feedforward(
            token_parts[index],
            attended[rows],
            heads_received[index],
            grad_parts[index],
            feedforward_norm2_gain,
            w_ffn,
            mixers,
        )

    fed = [feed(0), feed(1)]
    resid, h_two, act, grad_lift, grad_h2, mlp = [list(pair) for pair in zip(*fed)]
    gh_received = receive_own(grad_h2[0], grad_h2[1])
    join = lambda pair: jnp.concatenate(pair, axis=0)
    grad_rows_all = join(grad_parts)
    grad_down_full = matmul_low("td,tf->df", grad_rows_all, join(act))
    grad_up_full = matmul_low("td,th->dh", join(h_two), join(grad_lift))
    ffn_sums = jnp.concatenate([grad_up_full, grad_down_full], axis=1)
    ffn_part = scatter_sums(ffn_sums)

    residual_gradient, grad_resid_low, grad_attended, grad_other_heads, gain_second = middle(
        resid[0],
        grad_h2[0],
        gh_received,
        grad_parts[0],
        feedforward_norm2_gain,
        mixers,
        width,
        heads_width,
    )
    if lax.axis_size("tensor") == 2:
        grad_attended_other = swap_pairs(grad_other_heads)
    else:
        grad_attended_other = matmul_low(
            "td,dh->th", gather_rows(grad_resid_low)[1], mixers[:, :width]
        )
    mlp[1] = lax.optimization_barrier((mlp[1], grad_attended_other))[0]
    mlp_received = receive_own(mlp[0], mlp[1])
    grad_attended = join([grad_attended, grad_attended_other])
    attended_wide = jnp.concatenate([attended[:own_rows], heads_received[0]], axis=1)
    grad_out_wide = matmul_low("td,th->dh", grad_resid_low, attended_wide)
    out_sums = scatter_halving([grad_out_wide])

    pairs = width // (2 * DH)
    calls = 2 if pairs % 2 == 0 else 1
    grad_pieces, sums = [], []
    for call in range(calls):
        piece = attention_backward(
            queries,
            keys,
            values,
            grad_attended,
            attended,
            lse,
            tables,
            shift,
            rest_ids,
            call * (pairs // calls),
            pairs // calls,
        )
        grad_pieces.append(piece)
        columns = [matmul_low("td,tc->dc", h_one_all, jnp.concatenate(piece, axis=1))]
        sums.append(scatter_halving(columns))

    parts = [grad_pieces[call][which] for which in range(3) for call in range(calls)]
    grad_h1_other, gain_other = first_hidden(token_parts[1], w_qkv, parts, own_rows)
    grad_h1_own, gain_own = first_hidden(token_parts[0], w_qkv, parts, 0)
    first_hidden_gradient = grad_h1_own.astype(jnp.float32) + receive_own(
        grad_h1_own, grad_h1_other
    ).astype(jnp.float32)
    gain_grads = sum_everywhere(
        jnp.concatenate([gain_own + gain_other, gain_second], axis=0)
    )
    mixed = (
        resid[0]
        + (mlp[0].astype(jnp.float32) + mlp_received.astype(jnp.float32))
    ).astype(jnp.bfloat16)
    own_scaled1, inverse_deviation1 = normed[0]
    token_gradients = residual_gradient + norm_backward(
        first_hidden_gradient, own_scaled1, inverse_deviation1, attention_norm1_gain
    )
    ffn_part = ffn_part.astype(jnp.float32)
    qkv_part = jnp.concatenate(
        [
            part.reshape(shard_rows, 3, width // calls)
            for part in sums
        ],
        axis=2,
    )
    return (
        mixed,
        token_gradients,
        gain_grads[0],
        qkv_part,
        collect_heads(out_sums, width).T,
        gain_grads[1],
        ffn_part[:, : 2 * padded].reshape(shard_rows, 2, padded)[:, :, :hidden],
        ffn_part[:, 2 * padded : 2 * padded + hidden].T,
    )


def solution(mesh):
    return jax.shard_map(
        local,
        mesh=mesh,
        in_specs=(
            P(("dp", "tensor"), None),
            P("dp", None),
            P(),
            P("dp", None, "tensor"),
            P("tensor", "dp"),
            P(),
            P("dp", None, "tensor"),
            P("tensor", "dp"),
            P(("dp", "tensor"), None),
        ),
        out_specs=(
            P(("dp", "tensor"), None),
            P(("dp", "tensor"), None),
            P(),
            P("dp", None, "tensor"),
            P("tensor", "dp"),
            P(),
            P("dp", None, "tensor"),
            P("tensor", "dp"),
        ),
        check_vma=False,
    )
```
